32 devices in a mesh: section: 4 (over x, core), fsdp: 8 (over z, y).
Axes of the slice: x: 2, y: 2, z: 4, core: 2. Of those that a mesh axis runs over, the one named last changes fastest.
Arguments:
- produced: bfloat16 [4, 24, 256, 4096], P('section', 'fsdp'), may hold values from -6 to 6
- lengths: int32 [4, 24], P('section', 'fsdp'), may hold values from 64 to 256, as said below
- active: int32 [4, 24, 4], P('section', 'fsdp'), may hold values from 0 to 7, all different within a row
- window_blocks: int32 [8], replicated, may hold values from 0 to 249, as said below
- triplets: int32 [4, 8, 3], P('section'), may hold values from 0 to 23, as said below
- teacher: float32 [4, 8], P('section'), may hold values from -60 to 60
- norm_gain: bfloat16 [4096], P('fsdp'), may hold values from 0.5 to 1.5
- head: bfloat16 [32000, 4096], P(None, 'fsdp'), may hold values from -0.09375 to 0.09375
Outputs:
- losses: float32 [4], P('section')
- produced_grad: bfloat16 [4, 24, 256, 4096], P('section', 'fsdp')
- head_grad: float32 [1024, 4096], P(None, 'fsdp')
- gain_grad: float32 [4096], P('fsdp')
The draws below stay inside these ranges and needn't reach their ends.
Inputs may be any that keep to these rules, and one draw needn't show every extreme that they name: `lengths`: every device's first sequence holds 256 tokens, and some sequence holds 64. `active`: each row names 4 different slots. `window_blocks`: ids are distinct. `triplets`: each sequence of a group stands in exactly one triplet, once.
All inputs are finite; a program needn't handle non-finite values.
Results may differ from the reference program's by a relative error of at most 0.0051.
Values may be sent and summed in bfloat16 or wider, within the bound.
A program may use at most 192 MiB of HBM per device.

```python
import jax
import jax.numpy as jnp
from jax import lax

D = 4096
VOCAB = 32000
BLOCK = 128
U = 8
K = 4
LEN = 256
SEQ_DEV = 3
SECTIONS = 4
SEQS = 24
TRIPS = 8
NBLOCKS = 250


def draw_lengths(key, part):
    base = jax.random.randint(key, (SECTIONS, SEQS), LEN // 4, LEN + 1)
    index = jnp.arange(SEQS, dtype=jnp.int32)[None, :]
    base = jnp.where(index % SEQ_DEV == 0, LEN, base)
    return jnp.where(index == 1, LEN // 4, base).astype(jnp.int32)


def draw_window_blocks(key, part):
    others = jax.random.permutation(jax.random.fold_in(key, 1), NBLOCKS - 2)[:U - 2].astype(jnp.int32) + 1
    joined = jnp.concatenate([others, jnp.zeros((1,), jnp.int32), jnp.full((1,), NBLOCKS - 1, jnp.int32)])
    return jax.random.permutation(jax.random.fold_in(key, 2), joined).astype(jnp.int32)


def draw_triplets(key, part):
    section_keys = jax.random.split(jax.random.fold_in(key, 3), SECTIONS)
    orders = jax.vmap(lambda single: jax.random.permutation(single, SEQS))(section_keys)
    return orders.reshape(SECTIONS, TRIPS, 3).astype(jnp.int32)


def steps_of(key, shape, pieces, least, high):
    loudness, own = 1.0, jax.random.fold_in(key, 6)
    for dim, shards_of in pieces:
        heights = jnp.exp(jax.random.uniform(jax.random.fold_in(own, dim), (shards_of,), jnp.float32, least / len(pieces), high / len(pieces)))
        loudness = loudness * jnp.repeat(heights, shape[dim] // shards_of).reshape([-1 if axis == dim else 1 for axis in range(len(shape))])
    return loudness


def different_ones(key, rows, number_of, top, lift):
    order = jax.random.permutation(jax.random.fold_in(key, 1), number_of)
    boost = order
    for power in range(3):
        boost = boost * boost // number_of
    boost = boost * lift // number_of
    tickets = jax.random.randint(jax.random.fold_in(key, 2), (rows, number_of), 0, 4096) + boost
    holders = jax.random.permutation(jax.random.fold_in(key, 3), rows)[jnp.arange(number_of) % rows]
    tickets = jnp.where(jnp.arange(rows)[:, None] == holders[None, :], 1 << 14, tickets)
    merit = tickets * number_of + jnp.arange(number_of)
    return lax.top_k(merit.astype(jnp.int32), top)[1].astype(jnp.int32)


def bell_draw(key, shape, scale, bound, shards=(), kind=jnp.bfloat16):
    array = jax.random.normal(key, shape, jnp.float32) * scale
    if len(shards) > 0:
        array = steps_of(key, shape, shards, -0.22, 0.18) * array
    return jnp.clip(array, min=-bound, max=bound).astype(kind)


def setup_inputs(seed: int = 0) -> dict:
    seeds = jax.random.split(jax.random.key(seed), 9)
    produced = bell_draw(seeds[0], (SECTIONS, SEQS, LEN, D), 1.0, 6.0, ((0, 4), (1, 8)))
    lengths = draw_lengths(jax.random.fold_in(seeds[8], 71), 0)
    active = different_ones(seeds[2], SECTIONS * SEQS, U, K, 8192).reshape((SECTIONS, SEQS, K))
    window_blocks = draw_window_blocks(jax.random.fold_in(seeds[8], 71), 0)
    triplets = draw_triplets(jax.random.fold_in(seeds[8], 71), 0)
    teacher = bell_draw(seeds[5], (SECTIONS, TRIPS), 10.0, 60.0, ((0, 4),), jnp.float32)
    norm_gain = jnp.clip(1.0 + 0.1 * jax.random.normal(seeds[6], (D,), jnp.float32), 0.5, 1.5).astype(jnp.bfloat16)
    head = bell_draw(seeds[7], (VOCAB, D), D ** -0.5, 0.09375, ((1, 8),))
    return dict(produced=produced, lengths=lengths, active=active, window_blocks=window_blocks, triplets=triplets, teacher=teacher, norm_gain=norm_gain, head=head)


eps = 1e-05
loss_scale = 256.0

def pool_terms(logits):
    smooth = jax.nn.softplus(logits)
    return (jnp.log1p(smooth), jax.nn.sigmoid(logits) / (1.0 + smooth))

def reference(produced, lengths, active, window_blocks, triplets, teacher, norm_gain, head):
    offsets = jnp.arange(BLOCK, dtype=jnp.int32)
    block_rows = (window_blocks[:, None] * BLOCK + offsets[None, :]).reshape(-1).astype(jnp.int32)
    window = head[block_rows]
    gain32 = norm_gain.astype(jnp.float32)
    head_total = jnp.zeros((U * BLOCK, D), jnp.float32)
    gain_total = jnp.zeros((D,), jnp.float32)
    losses = []
    returned = [None] * SECTIONS
    position = jnp.arange(LEN, dtype=jnp.int32)
    slot_range = jnp.arange(U, dtype=jnp.int32)
    for target in range(SECTIONS):
        source = (target - 1) % SECTIONS
        hidden = produced[source].reshape(SEQS * LEN, D)
        seq_lengths = lengths[source]
        block_slots = active[source]
        widened = hidden.astype(jnp.float32)
        inv_rms = lax.rsqrt(lax.optimization_barrier(jnp.mean(widened * widened, axis=1, keepdims=True)) + eps)
        normed = (widened * inv_rms * gain32).astype(jnp.bfloat16)
        logits = jnp.dot(normed, window.T, preferred_element_type=jnp.float32).reshape(SEQS, LEN, U * BLOCK)
        values, slopes = pool_terms(logits)
        weight = (position[None, :] < seq_lengths[:, None]).astype(jnp.float32) / seq_lengths[:, None].astype(jnp.float32)
        chosen = lax.optimization_barrier(jnp.sum((block_slots[:, :, None] == slot_range[None, None, :]).astype(jnp.float32), axis=1))
        spread = jnp.repeat(chosen, BLOCK, axis=1)
        pooled = lax.optimization_barrier(jnp.sum(weight[:, :, None] * values, axis=1)) * spread
        triplet_rows = triplets[target]
        query_rows = pooled[triplet_rows[:, 0]]
        positive = pooled[triplet_rows[:, 1]]
        negative = pooled[triplet_rows[:, 2]]
        margin = lax.optimization_barrier(jnp.sum(query_rows * (positive - negative), axis=1))
        deviation = margin - teacher[target]
        losses.append(jnp.mean(deviation * deviation))
        grad_margin = loss_scale * 2.0 * deviation / TRIPS
        grad_pooled = jnp.zeros((SEQS, U * BLOCK), jnp.float32)
        grad_pooled = grad_pooled.at[triplet_rows[:, 0]].add(grad_margin[:, None] * (positive - negative))
        grad_pooled = grad_pooled.at[triplet_rows[:, 1]].add(grad_margin[:, None] * query_rows)
        grad_pooled = grad_pooled.at[triplet_rows[:, 2]].add(-(grad_margin[:, None] * query_rows))
        grad_values = grad_pooled * spread
        grad_logits = (weight[:, :, None] * grad_values[:, None, :] * slopes).astype(jnp.bfloat16)
        grad_logits = grad_logits.reshape(SEQS * LEN, U * BLOCK)
        grad_normed = jnp.dot(grad_logits, window, preferred_element_type=jnp.float32)
        head_total = head_total + jnp.dot(grad_logits.T, normed, preferred_element_type=jnp.float32)
        gain_total = gain_total + lax.optimization_barrier(jnp.sum(grad_normed * widened * inv_rms, axis=0))
        scaled = grad_normed * gain32
        grad_tokens = inv_rms * scaled - widened * (inv_rms * inv_rms * inv_rms) * lax.optimization_barrier(jnp.mean(scaled * widened, axis=1, keepdims=True))
        returned[source] = grad_tokens.astype(jnp.bfloat16).reshape(SEQS, LEN, D)
    return (jnp.stack(losses), jnp.stack(returned), head_total, gain_total)
```

```python
import jax
import jax.numpy as jnp
from jax import lax
from jax.experimental import pallas as pl
from jax.experimental.pallas import tpu as pltpu
from jax.sharding import PartitionSpec as P

D = 4096
BLOCK = 128
U = 8
K = 4
LEN = 256
SEQ_DEV = 3


eps = 1e-05
loss_scale = 256.0

MESH = pl.DeviceIdType.MESH
VMEM = pl.BlockSpec(memory_space=pltpu.VMEM)
SMEM = pl.BlockSpec(memory_space=pltpu.SMEM)
ANY = pl.BlockSpec(memory_space=pl.ANY)
bf16, f32 = jnp.bfloat16, jnp.float32


def greet(others):
    barrier = pltpu.get_barrier_semaphore()
    for device in others:
        pl.semaphore_signal(barrier, inc=1, device_id=device, device_id_type=MESH)
    pl.semaphore_wait(barrier, len(others))


def remote(src, dst, send, recv, device):
    return pltpu.make_async_remote_copy(
        src_ref=src,
        dst_ref=dst,
        send_sem=send,
        recv_sem=recv,
        device_id=device,
        device_id_type=MESH,
    )


def pick(hits, rows):
    return jnp.dot(hits, rows, precision=lax.Precision.HIGHEST, preferred_element_type=f32)


def collect_kernel(ids_ref, head_hbm, out_hbm, sems):
    copies = []
    for u in range(U):
        start = pl.multiple_of(ids_ref[u] * BLOCK, BLOCK)
        copies.append(
            pltpu.make_async_copy(
                head_hbm.at[pl.ds(start, BLOCK)],
                out_hbm.at[pl.ds(u * BLOCK, BLOCK)],
                sems.at[u],
            )
        )
    for copy in copies:
        copy.start()
    for copy in copies:
        copy.wait()


def collect_rows(ids, head):
    return pl.pallas_call(
        collect_kernel,
        name="collect_rows",
        out_shape=jax.ShapeDtypeStruct((U * BLOCK, head.shape[1]), head.dtype),
        in_specs=[SMEM, ANY],
        out_specs=ANY,
        scratch_shapes=[pltpu.SemaphoreType.DMA((U,))],
    )(ids, head)


ZA, YA, XA, MA, ML, ZC, YC, MC = 0, 1, 2, 4, 6, 8, 9, 10
GATHER_GROUPS = 12


def whole_kernel(
    n, piece_hbm, gain_ref, token_hbm, lens_ref, slots_ref, group_ref,
    loss_out, grad_hbm, head_out, gain_out,
    token_ref, normed_ref, window, logits, inv_ref, weight_ref, gains, got_group,
    pool_ref, held, grad_ref, loss_ref, gl, turned,
    mpart, opart, got_mate, sum_x, got_x, sum_yc, got_yc, sum_ya, got_ya,
    sum_zc, got_zc, sum_za, got_za, final_a, final_c, got_a, got_c,
    product, gain_row, gain_own, got_gain, gain_sum, got_sum,
    token_sem, own_sem, store_sem, wsend, wrecv, gsend, grecv, qsend, qrecv, psend, precv,
    msend, mrecv, rsend, rrecv, osend, orecv, tsend, trecv, ssend, srecv,
):
    s, f = lax.axis_index("section"), lax.axis_index("fsdp")
    core = lax.rem(s, 2)
    mate = s + 1 - 2 * core
    across = lax.rem(s + 2, 4)
    diagonal = lax.rem(mate + 2, 4)
    lines = n // 2
    a, b = lax.div(f, 2), lax.rem(f, 2)
    terms, columns = piece_hbm.shape
    tall, width = token_ref.shape
    peers = [(s, lax.rem(f + d, n)) for d in range(1, n)]
    sections = [(lax.rem(s + d, 4), f) for d in range(1, 4)]
    y_side = (s, 2 * a + 1 - b)
    greet(peers + sections)
    sent = []

    def push(src, dst, send, recv, device):
        copy = remote(src, dst, send, recv, device)
        copy.start()
        sent.append(copy)

    def arrive(spot, send, recv):
        remote(spot, spot, send, recv, (mate, f)).wait_recv()

    part_a, part_c = terms * 3 // 16, terms // 8
    first_c = 4 * part_a

    def rows_a(q):
        return pl.ds(pl.multiple_of(q * part_a, 16), part_a)

    def rows_c(c):
        return pl.ds(pl.multiple_of(first_c + c * part_c, 16), part_c)

    def wpush(src, g, rows, group, d, device):
        push(src, window.at[g, rows], wsend.at[group, d], wrecv.at[group, d], device)

    def warrive(g, rows, group, d):
        spot = window.at[g, rows]
        arrive(spot, wsend.at[group, d], wrecv.at[group, d])
        return spot

    def name(d, half):
        line = 2 * lax.rem(a - d + lines, lines)
        return line + (1 - b if half else b)

    mine_a, mine_c = rows_a(s), rows_c(core)
    along = [None] + [(s, 2 * lax.rem(a + d, lines) + b) for d in range(1, lines)]
    for d in range(1, lines):
        wpush(piece_hbm.at[mine_a], f, mine_a, ZA, d, along[d])
    wpush(piece_hbm.at[mine_a], f, mine_a, YA, 0, y_side)
    tokens = pltpu.make_async_copy(token_hbm, token_ref, token_sem)
    tokens.start()
    own = pltpu.make_async_copy(piece_hbm, window.at[f], own_sem)
    own.start()
    for d in range(1, n):
        push(gain_ref, gains.at[f], gsend.at[d], grecv.at[d], peers[d - 1])
    push(group_ref, got_group, qsend.at[0], qrecv.at[0], sections[2])
    for d in range(1, lines):
        wpush(piece_hbm.at[mine_c], f, mine_c, ZC, d, along[d])
    wpush(piece_hbm.at[mine_c], f, mine_c, YC, 0, y_side)
    gains[f] = gain_ref[...]

    def relay_a(d, half):
        g = name(d, half)
        spot = warrive(g, mine_a, YA if half else ZA, d)
        if not half:
            wpush(spot, g, mine_a, YA, d, y_side)
        wpush(spot, g, mine_a, XA + half, d, (across, f))
        wpush(spot, g, mine_a, MA + half, d, (mate, f))

    def relay_c(d, half):
        g = name(d, half)
        spot = warrive(g, mine_c, YC if half else ZC, d)
        if not half:
            wpush(spot, g, mine_c, YC, d, y_side)
        wpush(spot, g, mine_c, MC + half, d, (mate, f))

    def relay_x(d, half):
        g = name(d, half)
        spot = warrive(g, rows_a(across), XA + half, d)
        wpush(spot, g, rows_a(across), ML + half, d, (mate, f))

    def rows_of(i):
        return pl.ds(pl.multiple_of(i * LEN, LEN), LEN)

    def cols_of(g):
        return pl.ds(pl.multiple_of(g * columns, columns), columns)

    def measure_block(i, carry):
        squares = jnp.zeros((LEN, 1), f32)
        for g in range(n):
            wide = token_ref[rows_of(i), g * columns : (g + 1) * columns].astype(f32)
            squares = squares + jnp.sum(wide * wide, axis=1, keepdims=True)
        inv_ref[rows_of(i), :] = lax.rsqrt(squares / width + eps)
        count = lens_ref[i]
        inside = lax.broadcasted_iota(jnp.int32, (LEN, BLOCK), 0) < count
        weight_ref[rows_of(i), :] = jnp.where(inside, 1.0, 0.0) / count.astype(f32)
        return carry

    def norm_block(i, carry):
        inv = inv_ref[rows_of(i), :]
        for g in range(n):
            cols = slice(g * columns, (g + 1) * columns)
            wide = token_ref[rows_of(i), cols].astype(f32)
            normed_ref[rows_of(i), cols] = (wide * inv * gains[g]).astype(bf16)
        return carry

    def add_logits(start, size, g, fresh=False):
        places = pl.ds(start if isinstance(start, int) else pl.multiple_of(start, BLOCK), size)

        def block(i, carry):
            value = lax.dot_general(
                normed_ref[rows_of(i), cols_of(g)],
                window[g, places, :],
                (((1,), (1,)), ((), ())),
                preferred_element_type=f32,
            )
            if not fresh:
                value = value + logits[rows_of(i), places]
            logits[rows_of(i), places] = value
            return carry

        lax.fori_loop(0, SEQ_DEV, block, 0)

    chip = lax.div(s, 2)
    size_a, size_c = 2 * part_a, 2 * part_c

    def logits_a(d, half):
        g = name(d, half)
        warrive(g, rows_a(mate), MA + half, d)
        add_logits(chip * size_a, size_a, g)

    def logits_c(d, half):
        g = name(d, half)
        warrive(g, rows_c(1 - core), MC + half, d)
        add_logits(first_c, size_c, g)

    def logits_x(d, half):
        g = name(d, half)
        warrive(g, rows_a(diagonal), ML + half, d)
        add_logits((1 - chip) * size_a, size_a, g)

    def chosen(i, u):
        count = jnp.where(slots_ref[i * K] == u, 1.0, 0.0)
        for k in range(1, K):
            count = count + jnp.where(slots_ref[i * K + k] == u, 1.0, 0.0)
        return count

    def lanes(u):
        return pl.ds(pl.multiple_of(u * BLOCK, BLOCK), BLOCK)

    step = 64

    def pool_blocks(first, count):
        def tile(index, carry):
            u, i = first + lax.div(index, SEQ_DEV), lax.rem(index, SEQ_DEV)
            total = jnp.zeros((1, BLOCK), f32)
            for k in range(LEN // step):
                rows = pl.ds(pl.multiple_of(i * LEN + k * step, step), step)
                x = logits[rows, lanes(u)]
                weight = weight_ref[rows, :]
                e = jnp.exp(-jnp.abs(x))
                smooth = jnp.maximum(x, 0.0) + jnp.log1p(e)
                total = total + jnp.sum(weight * jnp.log1p(smooth), axis=0, keepdims=True)
                top = jnp.where(x >= 0.0, 1.0, e)
                logits[rows, lanes(u)] = weight * top / ((1.0 + e) * (1.0 + smooth))
            pool_ref[pl.ds(i * U + u, 1), :] = total * chosen(i, u)
            return carry

        lax.fori_loop(0, count * SEQ_DEV, tile, 0)

    tokens.wait()
    lax.fori_loop(0, SEQ_DEV, measure_block, 0)
    relay_a(0, 1)
    for d in range(1, lines):
        if d == 1:
            for k in range(1, n):
                spot = gains.at[lax.rem(f - k + n, n)]
                arrive(spot, gsend.at[k], grecv.at[k])
        relay_a(d, 0)
        if d <= SEQ_DEV:
            norm_block(d - 1, 0)
    for i in range(min(lines - 1, SEQ_DEV), SEQ_DEV):
        norm_block(i, 0)
    own.wait()
    add_logits(0, terms, f, fresh=True)
    logits_a(0, 1)
    for d in range(1, lines):
        relay_a(d, 1)
        logits_a(d, 0)
    relay_c(0, 1)
    for d in range(1, lines):
        relay_c(d, 0)
        logits_a(d, 1)
        if d == 1:
            relay_x(0, 1)
        relay_x(d, 0)
    pool_blocks(chip * size_a // BLOCK, size_a // BLOCK)
    logits_c(0, 1)
    for d in range(1, lines):
        relay_c(d, 1)
        logits_c(d, 0)
        relay_x(d, 1)
    for d in range(1, lines):
        logits_c(d, 1)
    pool_blocks(first_c // BLOCK, size_c // BLOCK)
    logits_x(0, 1)
    for d in range(1, lines):
        logits_x(d, 0)
    for d in range(1, lines):
        logits_x(d, 1)
    pool_blocks((1 - chip) * size_a // BLOCK, size_a // BLOCK)

    own_rows = SEQ_DEV * U
    for d in range(1, n):
        push(pool_ref, held.at[f], psend.at[d], precv.at[d], peers[d - 1])
    held[f] = pool_ref[...]
    arrive(got_group, qsend.at[0], qrecv.at[0])
    trips = group_ref.shape[0]
    lifted = trips * U
    group = jnp.broadcast_to(got_group[...][:, None, :], (trips, U, group_ref.shape[1]))
    group = group.reshape(lifted, group_ref.shape[1])
    within = lax.rem(lax.broadcasted_iota(jnp.int32, (lifted, 1), 0), U).astype(f32)
    aims = [group[:, k : k + 1] * U + within for k in range(3)]
    names = lax.broadcasted_iota(jnp.int32, (lifted, n * own_rows), 1).astype(f32)
    hits = [jnp.where(names == aims[k], 1.0, 0.0) for k in range(3)]
    own_names = lax.broadcasted_iota(jnp.int32, (lifted, BLOCK), 1)
    own_at = jnp.where(own_names < own_rows, own_names + f * own_rows, -1).astype(f32)
    own_hits = [jnp.where(own_at == aims[k], 1.0, 0.0) for k in range(3)]
    triple = lambda dim: lax.div(lax.broadcasted_iota(jnp.int32, (lifted, lifted), dim), U)
    same = jnp.where(triple(0) == triple(1), 1.0, 0.0)
    for d in range(1, n):
        arrive(held.at[lax.rem(f - d + n, n)], psend.at[d], precv.at[d])
    rows = held[...].reshape(n * own_rows, BLOCK)
    query = pick(hits[0], rows)
    gap = pick(hits[1] - hits[2], rows)
    margin = jnp.sum(pick(same, query * gap), axis=1, keepdims=True)
    deviation = margin - group[:, 3:4]
    loss = jnp.sum(deviation * deviation, axis=0, keepdims=True) / (trips * U)
    loss_ref[...] = jnp.broadcast_to(loss, loss_ref.shape)
    push(loss_ref, loss_out, qsend.at[1], qrecv.at[1], sections[0])
    grad_margin = loss_scale * 2.0 * deviation / trips
    back = (((0,), (0,)), ((), ()))
    grad = lax.dot_general(
        own_hits[0], grad_margin * gap, back,
        precision=lax.Precision.HIGHEST, preferred_element_type=f32,
    ) + lax.dot_general(
        own_hits[1] - own_hits[2], grad_margin * query, back,
        precision=lax.Precision.HIGHEST, preferred_element_type=f32,
    )
    grad_ref[...] = grad[:own_rows]

    def blocks_of(side_x, side_s, c):
        return [side_x, side_s, 4 + 2 * c, 5 + 2 * c]

    lists = [blocks_of(diagonal, mate, 1 - core), blocks_of(across, s, core)]
    for side in range(2):
        for p, u in enumerate(lists[side]):

            def turn(i, carry, u=u, p=p, side=side):
                row = grad_ref[pl.ds(i * U + u, 1), :] * chosen(i, u)
                value = logits[rows_of(i), lanes(u)] * row
                gl[rows_of(i), lanes(u)] = value.astype(bf16)
                turned[side, p * BLOCK : (p + 1) * BLOCK, rows_of(i)] = value.T.astype(bf16)
                return carry

            lax.fori_loop(0, SEQ_DEV, turn, 0)

    chunk = [lax.rem(a + 1 + d, lines) for d in range(lines)]
    tile = 2 * columns if 2 * columns < 256 else 256
    half_terms = terms // 2

    def multiply(side, d, out):
        def strip(j, carry):
            spot = pl.ds(pl.multiple_of(j * tile, tile), tile)
            source = pl.ds(pl.multiple_of(chunk[d] * 2 * columns + j * tile, tile), tile)
            out[d, :, spot] = jnp.dot(
                turned[side], normed_ref[:, source], preferred_element_type=f32
            ).astype(bf16)
            return carry

        lax.fori_loop(0, 2 * columns // tile, strip, 0)

    def to_mate(d):
        multiply(0, d, mpart)
        push(mpart.at[d], got_mate.at[d], msend.at[d], mrecv.at[d], (mate, f))

    def half(h):
        return pl.ds(pl.multiple_of(h * columns, columns), columns)

    r_x, r_a, r_c = slice(0, BLOCK), slice(BLOCK, 2 * BLOCK), slice(2 * BLOCK, 4 * BLOCK)
    RX, RYC, RYA, RZC, RZA = range(5)

    def rpush(src, dst, group, d, device):
        push(src, dst, rsend.at[group, d], rrecv.at[group, d], device)

    def rarrive(spot, group, d):
        arrive(spot, rsend.at[group, d], rrecv.at[group, d])

    def both(d, rows, cols):
        return opart[d, rows, cols].astype(f32) + got_mate[d, rows, cols].astype(f32)

    def stage_x(d):
        arrive(got_mate.at[d], msend.at[d], mrecv.at[d])
        sum_x[d] = both(d, r_x, slice(None)).astype(bf16)
        rpush(sum_x.at[d], got_x.at[d], RX, d, (across, f))
        sum_yc[d] = both(d, r_c, half(1 - b)).astype(bf16)
        rpush(sum_yc.at[d], got_yc.at[d], RYC, d, y_side)

    def stage_y(d):
        rarrive(got_x.at[d], RX, d)
        value = both(d, r_a, half(1 - b)) + got_x[d, :, half(1 - b)].astype(f32)
        sum_ya[d] = value.astype(bf16)
        rpush(sum_ya.at[d], got_ya.at[d], RYA, d, y_side)

    def stage_zc(d):
        rarrive(got_yc.at[d], RYC, d)
        value = both(d, r_c, half(b)) + got_yc[d].astype(f32)
        if d == lines - 1:
            return value
        sum_zc[d] = value.astype(bf16)
        rpush(sum_zc.at[d], got_zc.at[d], RZC, d, (s, 2 * chunk[d] + b))

    def stage_za(d):
        rarrive(got_ya.at[d], RYA, d)
        value = both(d, r_a, half(b)) + got_x[d, :, half(b)].astype(f32) + got_ya[d].astype(f32)
        if d == lines - 1:
            return value
        sum_za[d] = value.astype(bf16)
        rpush(sum_za.at[d], got_za.at[d], RZA, d, (s, 2 * chunk[d] + b))

    def store(i):
        spot = pl.ds(i * LEN, LEN)
        return pltpu.make_async_copy(token_ref.at[spot], grad_hbm.at[spot], store_sem.at[i])

    def token_block(i):
        spot = slice(i * LEN, (i + 1) * LEN)
        inv = inv_ref[spot, :]

        def strip(g, dots):
            value = jnp.dot(gl[spot, :], window[g], preferred_element_type=f32)
            wide = token_ref[spot, cols_of(g)].astype(f32)
            row = jnp.sum(value * wide * inv, axis=0, keepdims=True)
            gain_row[g] = row if i == 0 else gain_row[g] + row
            scaled = value * gains[g]
            product[:, cols_of(g)] = scaled
            return dots + jnp.sum(scaled * wide, axis=1, keepdims=True)

        dots = lax.fori_loop(0, n, strip, jnp.zeros((LEN, 1), f32))
        factor = inv * inv * inv * (dots / width)

        def finish(g, carry):
            wide = token_ref[spot, cols_of(g)].astype(f32)
            token_ref[spot, cols_of(g)] = (inv * product[:, cols_of(g)] - wide * factor).astype(bf16)
            return carry

        lax.fori_loop(0, n, finish, 0)
        store(i).start()

    to_mate(0)
    multiply(1, 0, opart)
    for d in range(1, lines):
        to_mate(d)
        stage_x(d - 1)
        multiply(1, d, opart)
    stage_x(lines - 1)
    token_block(0)
    stage_zc(0)
    stage_y(0)
    token_block(1)
    stage_zc(1)
    stage_y(1)
    stage_za(0)
    token_block(2)
    for d in range(1, n):
        device = peers[d - 1]
        push(gain_row.at[device[1]], got_gain.at[d], tsend.at[d], trecv.at[d], device)
    for d in range(2, lines):
        if d < lines - 1:
            stage_zc(d)
        stage_y(d)
        stage_za(d - 1)
    value_c = stage_zc(lines - 1)
    total = gain_row[f]
    for d in range(1, n):
        arrive(got_gain.at[d], tsend.at[d], trecv.at[d])
        total = total + got_gain[d]
    gain_sum[...] = total
    for d in range(1, 4):
        push(gain_sum, got_sum.at[d], ssend.at[d], srecv.at[d], sections[d - 1])
    for d in range(lines - 1):
        rarrive(got_zc.at[d], RZC, d)
        value_c = value_c + got_zc[d].astype(f32)
    final_c[...] = value_c.astype(bf16)
    push(final_c, got_c, osend.at[0], orecv.at[0], (across, f))
    value_a = stage_za(lines - 1)
    for d in range(lines - 1):
        rarrive(got_za.at[d], RZA, d)
        value_a = value_a + got_za[d].astype(f32)
    final_a[...] = value_a.astype(bf16)
    push(final_a, got_a.at[0], osend.at[1], orecv.at[1], (across, f))
    push(final_a, got_a.at[1], osend.at[2], orecv.at[2], (mate, f))

    def band(u, count=1):
        return pl.ds(pl.multiple_of(u * BLOCK, BLOCK), count * BLOCK)

    head_out[band(s), :] = final_a[...].astype(f32)
    arrive(got_c, osend.at[0], orecv.at[0])
    spot_c = head_out.at[band(4 + 2 * core, 2)]
    spot_c[...] = final_c[...].astype(f32) + got_c[...].astype(f32)
    push(spot_c, spot_c, osend.at[3], orecv.at[3], (mate, f))
    for d in range(1, 4):
        arrive(got_sum.at[d], ssend.at[d], srecv.at[d])
    gain_out[...] = gain_sum[...] + got_sum[1] + got_sum[2] + got_sum[3]
    arrive(got_a.at[1], osend.at[2], orecv.at[2])
    head_out[band(mate), :] = got_a[1].astype(f32)
    arrive(got_a.at[0], osend.at[1], orecv.at[1])
    push(got_a.at[0], got_a.at[2], osend.at[4], orecv.at[4], (mate, f))
    head_out[band(across), :] = got_a[0].astype(f32)
    arrive(head_out.at[band(6 - 2 * core, 2)], osend.at[3], orecv.at[3])
    arrive(got_a.at[2], osend.at[4], orecv.at[4])
    head_out[band(diagonal), :] = got_a[2].astype(f32)
    arrive(loss_out, qsend.at[1], qrecv.at[1])
    for i in range(SEQ_DEV):
        store(i).wait()
    for copy in sent:
        copy.wait_send()


def run_whole(piece, gain, tokens, lens, slots, group, n):
    terms, columns = piece.shape
    tall, width = tokens.shape
    lines = n // 2
    own_rows = SEQ_DEV * U
    half_terms = terms // 2

    def vm(*shape, dtype=bf16):
        return pltpu.VMEM(shape, dtype)

    def pair(*shape):
        return [pltpu.SemaphoreType.DMA(shape)] * 2

    scratch = [
        vm(tall, width), vm(tall, width), vm(n, terms, columns), vm(tall, terms, dtype=f32),
        vm(tall, 1, dtype=f32), vm(tall, BLOCK, dtype=f32), vm(n, 1, columns, dtype=f32),
        vm(*group.shape, dtype=f32),
        vm(own_rows, BLOCK, dtype=f32), vm(n, own_rows, BLOCK, dtype=f32),
        vm(own_rows, BLOCK, dtype=f32), vm(1, 128, dtype=f32),
        vm(tall, terms), vm(2, half_terms, tall),
        vm(lines, half_terms, 2 * columns), vm(lines, half_terms, 2 * columns),
        vm(lines, half_terms, 2 * columns),
        vm(lines, BLOCK, 2 * columns), vm(lines, BLOCK, 2 * columns),
        vm(lines, 2 * BLOCK, columns), vm(lines, 2 * BLOCK, columns),
        vm(lines, BLOCK, columns), vm(lines, BLOCK, columns),
        vm(lines, 2 * BLOCK, columns), vm(lines, 2 * BLOCK, columns),
        vm(lines, BLOCK, columns), vm(lines, BLOCK, columns),
        vm(BLOCK, columns), vm(2 * BLOCK, columns),
        vm(3, BLOCK, columns), vm(2 * BLOCK, columns),
        vm(LEN, width, dtype=f32), vm(n, 1, columns, dtype=f32), vm(1, columns, dtype=f32),
        vm(n, 1, columns, dtype=f32), vm(1, columns, dtype=f32), vm(4, 1, columns, dtype=f32),
        pltpu.SemaphoreType.DMA, pltpu.SemaphoreType.DMA, pltpu.SemaphoreType.DMA((SEQ_DEV,)),
    ]
    scratch += pair(GATHER_GROUPS, lines) + pair(n) + pair(2) + pair(n)
    scratch += pair(lines) + pair(5, lines) + pair(5) + pair(n) + pair(4)
    return pl.pallas_call(
        lambda *refs: whole_kernel(n, *refs),
        name="splade_step",
        out_shape=(
            jax.ShapeDtypeStruct((1, 128), f32),
            jax.ShapeDtypeStruct((tall, width), bf16),
            jax.ShapeDtypeStruct((terms, columns), f32),
            jax.ShapeDtypeStruct((1, columns), f32),
        ),
        in_specs=[ANY, VMEM, ANY, SMEM, SMEM, VMEM],
        out_specs=(VMEM, ANY, VMEM, VMEM),
        scratch_shapes=scratch,
        compiler_params=pltpu.CompilerParams(
            collective_id=0, has_side_effects=True, vmem_limit_bytes=62 << 20
        ),
    )(piece, gain, tokens, lens, slots, group)


def local(produced, lengths, active, window_blocks, triplets, teacher, norm_gain, head):
    shards = lax.axis_size("fsdp")
    columns = head.shape[1]
    group = jnp.concatenate([triplets[0].astype(f32), teacher[0][:, None]], axis=1)
    piece = collect_rows(window_blocks, head)
    gain = norm_gain.astype(f32)[None, :]
    tokens = produced.reshape(SEQ_DEV * LEN, D)
    loss_row, grad_tokens, head_grad, gain_grad = run_whole(
        piece, gain, tokens, lengths.reshape(-1), active.reshape(-1), group, shards
    )
    return (
        loss_row[0, :1],
        grad_tokens.reshape(1, SEQ_DEV, LEN, D),
        head_grad,
        gain_grad.reshape(columns),
    )


def solution(mesh):
    return jax.shard_map(
        local,
        mesh=mesh,
        in_specs=(
            P("section", "fsdp", None, None),
            P("section", "fsdp"),
            P("section", "fsdp", None),
            P(),
            P("section", None, None),
            P("section", None),
            P("fsdp"),
            P(None, "fsdp"),
        ),
        out_specs=(P("section"), P("section", "fsdp", None, None), P(None, "fsdp"), P("fsdp")),
        check_vma=False,
    )
```

```python
import jax
import jax.numpy as jnp
from jax import lax
from jax.experimental import pallas as pl
from jax.experimental.pallas import tpu as pltpu
from jax.sharding import PartitionSpec as P

D = 4096
BLOCK = 128
U = 8
K = 4
LEN = 256
SEQ_DEV = 3


eps = 1e-05
loss_scale = 256.0

MESH = pl.DeviceIdType.MESH
VMEM = pl.BlockSpec(memory_space=pltpu.VMEM)
SMEM = pl.BlockSpec(memory_space=pltpu.SMEM)
ANY = pl.BlockSpec(memory_space=pl.ANY)
bf16, f32 = jnp.bfloat16, jnp.float32


def greet(others):
    barrier = pltpu.get_barrier_semaphore()
    for device in others:
        pl.semaphore_signal(barrier, inc=1, device_id=device, device_id_type=MESH)
    pl.semaphore_wait(barrier, len(others))


def remote(src, dst, send, recv, device):
    return pltpu.make_async_remote_copy(
        src_ref=src,
        dst_ref=dst,
        send_sem=send,
        recv_sem=recv,
        device_id=device,
        device_id_type=MESH,
    )


def pick(hits, rows):
    return jnp.dot(hits, rows, precision=lax.Precision.HIGHEST, preferred_element_type=f32)


def collect_kernel(ids_ref, head_hbm, out_ref, sems):
    copies = []
    for u in range(U):
        start = pl.multiple_of(ids_ref[u] * BLOCK, BLOCK)
        copies.append(
            pltpu.make_async_copy(
                head_hbm.at[pl.ds(start, BLOCK)],
                out_ref.at[pl.ds(u * BLOCK, BLOCK)],
                sems.at[u],
            )
        )
    for copy in copies:
        copy.start()
    for copy in copies:
        copy.wait()


def collect_rows(ids, head):
    return pl.pallas_call(
        collect_kernel,
        name="collect_rows",
        out_shape=jax.ShapeDtypeStruct((U * BLOCK, head.shape[1]), head.dtype),
        in_specs=[SMEM, ANY],
        out_specs=VMEM,
        scratch_shapes=[pltpu.SemaphoreType.DMA((U,))],
    )(ids, head)


ZA, YA, XA, MA, ML, ZC, YC, MC = 0, 1, 2, 4, 6, 8, 9, 10
GATHER_GROUPS = 12


def whole_kernel(
    n, piece_hbm, gain_ref, token_hbm, lens_ref, slots_ref, group_ref,
    loss_out, grad_hbm, head_out, gain_out,
    token_ref, normed_ref, window, logits, inv_ref, weight_ref, gains, got_group,
    pool_ref, held, grad_ref, loss_ref, gl, turned,
    mpart, opart, got_mate, sum_x, got_x, sum_yc, got_yc, sum_ya, got_ya,
    sum_zc, got_zc, sum_za, got_za, total_a, total_c, dots_ref, final_a, final_c, got_a, got_c,
    product, gain_row, gain_own, got_gain, gain_sum, got_sum,
    token_sem, own_sem, store_sem, wsend, wrecv, gsend, grecv, qsend, qrecv, psend, precv,
    msend, mrecv, rsend, rrecv, osend, orecv, tsend, trecv, ssend, srecv,
):
    s, f = lax.axis_index("section"), lax.axis_index("fsdp")
    core = lax.rem(s, 2)
    mate = s + 1 - 2 * core
    across = lax.rem(s + 2, 4)
    diagonal = lax.rem(mate + 2, 4)
    lines = n // 2
    a, b = lax.div(f, 2), lax.rem(f, 2)
    terms, columns = piece_hbm.shape
    tall, width = token_ref.shape
    half_terms = terms // 2
    peers = [(s, lax.rem(f + d, n)) for d in range(1, n)]
    sections = [(lax.rem(s + d, 4), f) for d in range(1, 4)]
    y_side = (s, 2 * a + 1 - b)
    own = pltpu.make_async_copy(piece_hbm, window.at[f], own_sem)
    own.start()
    tokens = pltpu.make_async_copy(token_hbm, token_ref, token_sem)
    tokens.start()
    greet(peers + sections)
    sent = []

    def push(src, dst, send, recv, device, valid=None):
        copy = remote(src, dst, send, recv, device)
        if valid is None:
            copy.start()
        else:
            pl.when(valid)(copy.start)
        sent.append((copy, valid))

    def arrive(spot, send, recv):
        remote(spot, spot, send, recv, (mate, f)).wait_recv()

    part_a, part_c = terms * 3 // 16, terms // 8
    first_c = 4 * part_a

    def rows_a(q):
        return pl.ds(pl.multiple_of(q * part_a, 16), part_a)

    def rows_c(c):
        return pl.ds(pl.multiple_of(first_c + c * part_c, 16), part_c)

    def wpush(src, g, rows, group, q, device, valid=None):
        push(src, window.at[g, rows], wsend.at[group, q], wrecv.at[group, q], device, valid)

    def warrive(g, rows, group, q):
        spot = window.at[g, rows]
        arrive(spot, wsend.at[group, q], wrecv.at[group, q])
        return spot

    paired = jnp.minimum(a, lines - 1 - a)
    line, lower = [a], [0]
    for d in range(1, lines):
        below = jnp.where(d <= 2 * paired, d % 2, jnp.where(2 * a > lines - 1, 1, 0))
        distance = jnp.where(d <= 2 * paired, (d + 1) // 2, d - paired)
        line.append(a + (1 - 2 * below) * distance)
        lower.append(below)

    def name(d, half):
        return 2 * line[d] + (1 - b if half else b)

    def step_to(place):
        valid = (place >= 0) & (place < lines)
        return (s, 2 * lax.rem(place + lines, lines) + b), valid

    mine_a, mine_c = rows_a(s), rows_c(core)

    def begin(mine, group_z, group_y):
        src = window.at[f, mine]
        for place in (a - 1, a + 1):
            device, valid = step_to(place)
            wpush(src, f, mine, group_z, a, device, valid)
        wpush(src, f, mine, group_y, a, y_side)

    own.wait()
    begin(mine_a, ZA, YA)
    gains[f] = gain_ref[...].astype(f32)
    for d in range(1, n):
        push(gains.at[f], gains.at[f], gsend.at[d], grecv.at[d], peers[d - 1])
    push(group_ref, got_group, qsend.at[0], qrecv.at[0], sections[2])

    def relay(d, half, mine, group_z, group_y, group_m):
        g, q = name(d, half), line[d]
        spot = warrive(g, mine, group_y if half else group_z, q)
        if not half:
            device, valid = step_to(a + 2 * lower[d] - 1)
            wpush(spot, g, mine, group_z, q, device, valid)
            wpush(spot, g, mine, group_y, q, y_side)
        if group_m == MA:
            wpush(spot, g, mine, XA + half, q, (across, f))
        wpush(spot, g, mine, group_m + half, q, (mate, f))

    def relay_a(d, half):
        relay(d, half, mine_a, ZA, YA, MA)

    def relay_c(d, half):
        relay(d, half, mine_c, ZC, YC, MC)

    def relay_x(d, half):
        g, q = name(d, half), line[d]
        spot = warrive(g, rows_a(across), XA + half, q)
        wpush(spot, g, rows_a(across), ML + half, q, (mate, f))

    def rows_of(i):
        return pl.ds(pl.multiple_of(i * LEN, LEN), LEN)

    def cols_of(g):
        return pl.ds(pl.multiple_of(g * columns, columns), columns)

    def measure_block(i, carry):
        squares = jnp.zeros((LEN, 1), f32)
        for g in range(n):
            wide = token_ref[rows_of(i), g * columns : (g + 1) * columns].astype(f32)
            squares = squares + jnp.sum(wide * wide, axis=1, keepdims=True)
        inv_ref[rows_of(i), :] = lax.rsqrt(squares / width + eps)
        count = lens_ref[0, i]
        inside = lax.broadcasted_iota(jnp.int32, (LEN, BLOCK), 0) < count
        weight_ref[rows_of(i), :] = jnp.where(inside, 1.0, 0.0) / count.astype(f32)
        return carry

    def norm_block(i, carry):
        inv = inv_ref[rows_of(i), :]
        for g in range(n):
            cols = slice(g * columns, (g + 1) * columns)
            wide = token_ref[rows_of(i), cols].astype(f32)
            normed_ref[rows_of(i), cols] = (wide * inv * gains[g]).astype(bf16)
        return carry

    def add_logits(start, size, pieces, fresh=False):
        places = pl.ds(start if isinstance(start, int) else pl.multiple_of(start, BLOCK), size)
        value = None
        for g in pieces:
            part = lax.dot_general(
                normed_ref[:, cols_of(g)],
                window[g, places, :],
                (((1,), (1,)), ((), ())),
                preferred_element_type=f32,
            )
            value = part if value is None else value + part
        logits[:, places] = value if fresh else value + logits[:, places]

    chip = lax.div(s, 2)
    size_a, size_c = 2 * part_a, 2 * part_c

    def logits_of(pieces, start, size, rows, group):
        for d, half in pieces:
            warrive(name(d, half), rows, group + half, line[d])
        add_logits(start, size, [name(d, half) for d, half in pieces])

    def logits_a(*pieces):
        logits_of(pieces, chip * size_a, size_a, rows_a(mate), MA)

    def logits_c(*pieces):
        logits_of(pieces, first_c, size_c, rows_c(1 - core), MC)

    def logits_x(*pieces):
        logits_of(pieces, (1 - chip) * size_a, size_a, rows_a(diagonal), ML)

    def chosen(i, u):
        count = jnp.where(slots_ref[0, i, 0] == u, 1.0, 0.0)
        for k in range(1, K):
            count = count + jnp.where(slots_ref[0, i, k] == u, 1.0, 0.0)
        return count

    def lanes(u):
        return pl.ds(pl.multiple_of(u * BLOCK, BLOCK), BLOCK)

    step = 64

    def pool_blocks(first, count):
        def tile(index, carry):
            u, i = first + lax.div(index, SEQ_DEV), lax.rem(index, SEQ_DEV)
            total = jnp.zeros((1, BLOCK), f32)
            for k in range(LEN // step):
                rows = pl.ds(pl.multiple_of(i * LEN + k * step, step), step)
                x = logits[rows, lanes(u)]
                weight = weight_ref[rows, :]
                e = jnp.exp(-jnp.abs(x))
                smooth = jnp.maximum(x, 0.0) + jnp.log1p(e)
                total = total + jnp.sum(weight * jnp.log1p(smooth), axis=0, keepdims=True)
                top = jnp.where(x >= 0.0, 1.0, e)
                logits[rows, lanes(u)] = weight * top / ((1.0 + e) * (1.0 + smooth))
            pool_ref[pl.ds(i * U + u, 1), :] = total * chosen(i, u)
            return carry

        lax.fori_loop(0, count * SEQ_DEV, tile, 0)

    tokens.wait()
    lax.fori_loop(0, SEQ_DEV, measure_block, 0)
    relay_a(0, 1)
    relay_a(1, 0)
    for k in range(1, n):
        arrive(gains.at[lax.rem(f - k + n, n)], gsend.at[k], grecv.at[k])
    for d in range(2, lines):
        norm_block(d - 2, 0) if d < 2 + SEQ_DEV else None
        relay_a(d, 0)
        relay_a(d - 1, 1)
    begin(mine_c, ZC, YC)
    for i in range(lines - 2, SEQ_DEV):
        norm_block(i, 0)
    relay_a(lines - 1, 1)
    for j in range(2):
        add_logits(j * half_terms, half_terms, [f], fresh=True)
    logits_a((0, 1), (1, 0))
    relay_c(1, 0)
    relay_c(0, 1)
    for d in range(2, lines):
        logits_a((d, 0), (d - 1, 1))
        relay_c(d, 0)
        relay_c(d - 1, 1)
    logits_a((lines - 1, 1))
    relay_x(0, 1)
    relay_x(1, 0)
    pool_blocks(chip * size_a // BLOCK, size_a // BLOCK)
    relay_c(lines - 1, 1)
    for d in range(2, lines):
        relay_x(d, 0)
        relay_x(d - 1, 1)
        if d == 2:
            logits_c((0, 1), (1, 0))
        logits_c((d, 0), (d - 1, 1))
    logits_c((lines - 1, 1))
    logits_x((0, 1), (1, 0))
    pool_blocks(first_c // BLOCK, size_c // BLOCK)
    for d in range(2, lines - 1):
        logits_x((d, 0), (d - 1, 1))
    relay_x(lines - 1, 1)
    logits_x((lines - 1, 0), (lines - 2, 1), (lines - 1, 1))
    pool_blocks((1 - chip) * size_a // BLOCK, size_a // BLOCK)

    own_rows = SEQ_DEV * U
    for d in range(1, n):
        push(pool_ref, held.at[f], psend.at[d], precv.at[d], peers[d - 1])
    held[f] = pool_ref[...]
    arrive(got_group, qsend.at[0], qrecv.at[0])
    trips = group_ref.shape[0]
    lifted = trips * U
    group = jnp.broadcast_to(got_group[...][:, None, :], (trips, U, group_ref.shape[1]))
    group = group.reshape(lifted, group_ref.shape[1])
    within = lax.rem(lax.broadcasted_iota(jnp.int32, (lifted, 1), 0), U).astype(f32)
    aims = [group[:, k : k + 1] * U + within for k in range(3)]
    names = lax.broadcasted_iota(jnp.int32, (lifted, n * own_rows), 1).astype(f32)
    hits = [jnp.where(names == aims[k], 1.0, 0.0) for k in range(3)]
    own_names = lax.broadcasted_iota(jnp.int32, (lifted, BLOCK), 1)
    own_at = jnp.where(own_names < own_rows, own_names + f * own_rows, -1).astype(f32)
    own_hits = [jnp.where(own_at == aims[k], 1.0, 0.0) for k in range(3)]
    triple = lambda dim: lax.div(lax.broadcasted_iota(jnp.int32, (lifted, lifted), dim), U)
    same = jnp.where(triple(0) == triple(1), 1.0, 0.0)
    for d in range(1, n):
        arrive(held.at[lax.rem(f - d + n, n)], psend.at[d], precv.at[d])
    rows = held[...].reshape(n * own_rows, BLOCK)
    query = pick(hits[0], rows)
    gap = pick(hits[1] - hits[2], rows)
    margin = jnp.sum(pick(same, query * gap), axis=1, keepdims=True)
    deviation = margin - group[:, 3:4]
    loss = jnp.sum(deviation * deviation, axis=0, keepdims=True) / (trips * U)
    loss_ref[...] = jnp.broadcast_to(loss, loss_ref.shape)
    push(loss_ref, loss_out, qsend.at[1], qrecv.at[1], sections[0])
    grad_margin = loss_scale * 2.0 * deviation / trips
    back = (((0,), (0,)), ((), ()))
    grad = lax.dot_general(
        own_hits[0], grad_margin * gap, back,
        precision=lax.Precision.HIGHEST, preferred_element_type=f32,
    ) + lax.dot_general(
        own_hits[1] - own_hits[2], grad_margin * query, back,
        precision=lax.Precision.HIGHEST, preferred_element_type=f32,
    )
    grad_ref[...] = grad[:own_rows]

    def blocks_of(side_x, side_s, c):
        return [side_x, side_s, 4 + 2 * c, 5 + 2 * c]

    lists = [blocks_of(diagonal, mate, 1 - core), blocks_of(across, s, core)]
    for side in range(2):
        for p, u in enumerate(lists[side]):

            def turn(i, carry, u=u, p=p, side=side):
                row = grad_ref[pl.ds(i * U + u, 1), :] * chosen(i, u)
                value = logits[rows_of(i), lanes(u)] * row
                gl[rows_of(i), lanes(u)] = value.astype(bf16)
                turned[side, p * BLOCK : (p + 1) * BLOCK, rows_of(i)] = value.T.astype(bf16)
                return carry

            lax.fori_loop(0, SEQ_DEV, turn, 0)

    chunk = line[:0:-1] + [a]
    rising = [1 - x for x in lower[:0:-1]]
    tile = 2 * columns if 2 * columns < 1024 else 1024
    def multiply(side, d, rows, out):
        def strip(j, carry):
            spot = pl.ds(pl.multiple_of(j * tile, tile), tile)
            source = pl.ds(pl.multiple_of(chunk[d] * 2 * columns + j * tile, tile), tile)
            out[d, rows, spot] = jnp.dot(
                turned[side, rows, :], normed_ref[:, source], preferred_element_type=f32
            ).astype(bf16)
            return carry

        lax.fori_loop(0, 2 * columns // tile, strip, 0)

    def to_mate(d, rows, kind):
        multiply(0, d, rows, mpart)
        push(
            mpart.at[d, rows], got_mate.at[d, rows],
            msend.at[kind, d], mrecv.at[kind, d], (mate, f),
        )

    def from_mate(d, rows, kind):
        arrive(got_mate.at[d, rows], msend.at[kind, d], mrecv.at[kind, d])

    def half(h):
        return pl.ds(pl.multiple_of(h * columns, columns), columns)

    r_x, r_a, r_c = slice(0, BLOCK), slice(BLOCK, 2 * BLOCK), slice(2 * BLOCK, 4 * BLOCK)
    RX, RYC, RYA, RZC, RZA = range(5)

    def rpush(src, dst, group, d, device):
        push(src, dst, rsend.at[group, d], rrecv.at[group, d], device)

    def rarrive(spot, group, d):
        arrive(spot, rsend.at[group, d], rrecv.at[group, d])

    def both(d, rows, cols):
        return opart[d, rows, cols].astype(f32) + got_mate[d, rows, cols].astype(f32)

    def stage_x(d):
        from_mate(d, r_x, 0)
        sum_x[d] = both(d, r_x, slice(None)).astype(bf16)
        rpush(sum_x.at[d], got_x.at[d], RX, d, (across, f))

    def stage_c(d):
        from_mate(d, r_c, 2)
        sum_yc[d] = both(d, r_c, half(1 - b)).astype(bf16)

    def push_c(d):
        rpush(sum_yc.at[d], got_yc.at[d], RYC, d, y_side)

    def await_c(d):
        rarrive(got_yc.at[d], RYC, d)

    def stage_y(d):
        from_mate(d, r_a, 1)
        rarrive(got_x.at[d], RX, d)
        value = both(d, r_a, half(1 - b)) + got_x[d, :, half(1 - b)].astype(f32)
        sum_ya[d] = value.astype(bf16)
        rpush(sum_ya.at[d], got_ya.at[d], RYA, d, y_side)

    def along_z(d, value, out, got, group):
        q, way = chunk[d], 2 * rising[d] - 1
        before = a - way
        comes = (before >= 0) & (before < lines)

        @pl.when(comes)
        def _():
            rarrive(got.at[q], group, q)
            out[d] = (value + got[q].astype(f32)).astype(bf16)

        @pl.when(jnp.logical_not(comes))
        def _():
            out[d] = value.astype(bf16)

        last = jnp.where(a + way == q, 1 - rising[d], 0)
        slot = q + last * (lines - q)
        device = (s, 2 * (a + way) + b)
        push(out.at[d], got.at[slot], rsend.at[group, d], rrecv.at[group, slot], device)

    def end_z(got, total, group):
        for valid, slot in ((a > 0, a), (a < lines - 1, lines)):

            @pl.when(valid)
            def _(slot=slot):
                rarrive(got.at[slot], group, slot)
                total[...] += got[slot].astype(f32)

    def stage_zc(d):
        value = both(d, r_c, half(b)) + got_yc[d].astype(f32)
        if d == lines - 1:
            total_c[...] = value
        else:
            along_z(d, value, sum_zc, got_zc, RZC)

    def stage_za(d):
        rarrive(got_ya.at[d], RYA, d)
        value = both(d, r_a, half(b)) + got_x[d, :, half(b)].astype(f32) + got_ya[d].astype(f32)
        if d == lines - 1:
            total_a[...] = value
        else:
            along_z(d, value, sum_za, got_za, RZA)

    def store(i):
        spot = pl.ds(i * LEN, LEN)
        return pltpu.make_async_copy(token_ref.at[spot], grad_hbm.at[spot], store_sem.at[i])

    def token_strips(i, first, count):
        spot = slice(i * LEN, (i + 1) * LEN)
        inv = inv_ref[spot, :]

        def strip(j, dots):
            for g in (first + 2 * j, first + 2 * j + 1):
                value = jnp.dot(gl[spot, :], window[g], preferred_element_type=f32)
                wide = token_ref[spot, cols_of(g)].astype(f32)
                row = jnp.sum(value * wide * inv, axis=0, keepdims=True)
                gain_row[g] = row if i == 0 else gain_row[g] + row
                scaled = value * gains[g]
                product[:, cols_of(g)] = scaled
                dots = dots + jnp.sum(scaled * wide, axis=1, keepdims=True)
            return dots

        start = dots_ref[...] if first else jnp.zeros((LEN, 1), f32)
        dots_ref[...] = lax.fori_loop(0, count // 2, strip, start)

    def token_finish(i):
        spot = slice(i * LEN, (i + 1) * LEN)
        inv = inv_ref[spot, :]
        factor = inv * inv * inv * (dots_ref[...] / width)

        def finish(g, carry):
            wide = token_ref[spot, cols_of(g)].astype(f32)
            token_ref[spot, cols_of(g)] = (inv * product[:, cols_of(g)] - wide * factor).astype(bf16)
            return carry

        lax.fori_loop(0, n, finish, 0)
        store(i).start()

    for d in range(lines):
        to_mate(d, r_x, 0)
    to_mate(0, r_c, 2)
    for d in range(lines):
        multiply(1, d, r_x, opart)
        stage_x(d)
    multiply(1, 0, r_c, opart)
    stage_c(0)
    push_c(0)
    for d in range(1, lines):
        to_mate(d, r_c, 2)
        multiply(1, d, r_c, opart)
        stage_c(d)
        if d == 1:
            push_c(1)
            for k in range(lines):
                to_mate(k, r_a, 1)
                multiply(1, k, r_a, opart)
    for d in range(2, lines):
        await_c(d - 2)
        push_c(d)
        if d == 2:
            token_strips(0, 0, lines)
        if d == 3:
            token_strips(0, lines, lines)
            token_finish(0)
        stage_zc(d - 2)
    for d in range(lines // 2):
        stage_y(d)
    token_strips(1, 0, n)
    token_finish(1)
    await_c(lines - 2)
    stage_zc(lines - 2)
    for d in range(lines // 2, lines):
        stage_y(d)
    stage_za(0)
    token_strips(2, 0, n)
    token_finish(2)
    for d in range(1, n):
        device = peers[d - 1]
        push(gain_row.at[device[1]], got_gain.at[d], tsend.at[d], trecv.at[d], device)
    await_c(lines - 1)
    stage_zc(lines - 1)
    for d in range(1, lines - 2):
        stage_za(d)
    end_z(got_zc, total_c, RZC)
    final_c[...] = total_c[...].astype(bf16)
    push(final_c, got_c, osend.at[0], orecv.at[0], (across, f))
    stage_za(lines - 2)
    total = gain_row[f]
    for d in range(1, n):
        arrive(got_gain.at[d], tsend.at[d], trecv.at[d])
        total = total + got_gain[d]
    gain_sum[...] = total
    for d in range(1, 4):
        push(gain_sum, got_sum.at[d], ssend.at[d], srecv.at[d], sections[d - 1])
    stage_za(lines - 1)
    end_z(got_za, total_a, RZA)
    final_a[...] = total_a[...].astype(bf16)
    push(final_a, got_a.at[0], osend.at[1], orecv.at[1], (across, f))
    push(final_a, got_a.at[1], osend.at[2], orecv.at[2], (mate, f))

    def band(u, count=1):
        return pl.ds(pl.multiple_of(u * BLOCK, BLOCK), count * BLOCK)

    head_out[band(s), :] = final_a[...].astype(f32)
    arrive(got_c, osend.at[0], orecv.at[0])
    spot_c = head_out.at[band(4 + 2 * core, 2)]
    spot_c[...] = final_c[...].astype(f32) + got_c[...].astype(f32)
    push(spot_c, spot_c, osend.at[3], orecv.at[3], (mate, f))
    for d in range(1, 4):
        arrive(got_sum.at[d], ssend.at[d], srecv.at[d])
    gain_out[...] = gain_sum[...] + got_sum[1] + got_sum[2] + got_sum[3]
    arrive(got_a.at[1], osend.at[2], orecv.at[2])
    head_out[band(mate), :] = got_a[1].astype(f32)
    arrive(got_a.at[0], osend.at[1], orecv.at[1])
    push(got_a.at[0], got_a.at[2], osend.at[4], orecv.at[4], (mate, f))
    head_out[band(across), :] = got_a[0].astype(f32)
    arrive(head_out.at[band(6 - 2 * core, 2)], osend.at[3], orecv.at[3])
    arrive(got_a.at[2], osend.at[4], orecv.at[4])
    head_out[band(diagonal), :] = got_a[2].astype(f32)
    arrive(loss_out, qsend.at[1], qrecv.at[1])
    for i in range(SEQ_DEV):
        store(i).wait()
    for copy, valid in sent:
        if valid is None:
            copy.wait_send()
        else:
            pl.when(valid)(copy.wait_send)


def run_whole(piece, gain, tokens, lens, slots, group, n):
    terms, columns = piece.shape
    tall, width = tokens.shape
    lines = n // 2
    own_rows = SEQ_DEV * U
    half_terms = terms // 2

    def vm(*shape, dtype=bf16):
        return pltpu.VMEM(shape, dtype)

    def pair(*shape):
        return [pltpu.SemaphoreType.DMA(shape)] * 2

    scratch = [
        vm(tall, width), vm(tall, width), vm(n, terms, columns), vm(tall, terms, dtype=f32),
        vm(tall, 1, dtype=f32), vm(tall, BLOCK, dtype=f32), vm(n, 1, columns, dtype=f32),
        vm(*group.shape, dtype=f32),
        vm(own_rows, BLOCK, dtype=f32), vm(n, own_rows, BLOCK, dtype=f32),
        vm(own_rows, BLOCK, dtype=f32), vm(1, 128, dtype=f32),
        vm(tall, terms), vm(2, half_terms, tall),
        vm(lines, half_terms, 2 * columns), vm(lines, half_terms, 2 * columns),
        vm(lines, half_terms, 2 * columns),
        vm(lines, BLOCK, 2 * columns), vm(lines, BLOCK, 2 * columns),
        vm(lines, 2 * BLOCK, columns), vm(lines, 2 * BLOCK, columns),
        vm(lines, BLOCK, columns), vm(lines, BLOCK, columns),
        vm(lines, 2 * BLOCK, columns), vm(lines + 1, 2 * BLOCK, columns),
        vm(lines, BLOCK, columns), vm(lines + 1, BLOCK, columns),
        vm(BLOCK, columns, dtype=f32), vm(2 * BLOCK, columns, dtype=f32), vm(LEN, 1, dtype=f32),
        vm(BLOCK, columns), vm(2 * BLOCK, columns),
        vm(3, BLOCK, columns), vm(2 * BLOCK, columns),
        vm(LEN, width, dtype=f32), vm(n, 1, columns, dtype=f32), vm(1, columns, dtype=f32),
        vm(n, 1, columns, dtype=f32), vm(1, columns, dtype=f32), vm(4, 1, columns, dtype=f32),
        pltpu.SemaphoreType.DMA, pltpu.SemaphoreType.DMA, pltpu.SemaphoreType.DMA((SEQ_DEV,)),
    ]
    scratch += pair(GATHER_GROUPS, lines) + pair(n) + pair(2) + pair(n)
    scratch += pair(3, lines) + pair(5, lines + 1) + pair(5) + pair(n) + pair(4)
    return pl.pallas_call(
        lambda *refs: whole_kernel(n, *refs),
        name="splade_step",
        out_shape=(
            jax.ShapeDtypeStruct((1, 128), f32),
            jax.ShapeDtypeStruct((tall, width), bf16),
            jax.ShapeDtypeStruct((terms, columns), f32),
            jax.ShapeDtypeStruct((1, columns), f32),
        ),
        in_specs=[ANY, VMEM, ANY, SMEM, SMEM, VMEM],
        out_specs=(VMEM, ANY, VMEM, VMEM),
        scratch_shapes=scratch,
        compiler_params=pltpu.CompilerParams(
            collective_id=0, has_side_effects=True, vmem_limit_bytes=62 << 20
        ),
    )(piece, gain, tokens, lens, slots, group)


def local(produced, lengths, active, window_blocks, triplets, teacher, norm_gain, head):
    shards = lax.axis_size("fsdp")
    columns = head.shape[1]
    group = jnp.concatenate([triplets[0].astype(f32), teacher[0][:, None]], axis=1)
    piece = collect_rows(window_blocks, head)
    gain = norm_gain[None, :]
    tokens = produced.reshape(SEQ_DEV * LEN, D)
    loss_row, grad_tokens, head_grad, gain_grad = run_whole(
        piece, gain, tokens, lengths, active, group, shards
    )
    return (
        loss_row[0, :1],
        grad_tokens.reshape(1, SEQ_DEV, LEN, D),
        head_grad,
        gain_grad.reshape(columns),
    )


def solution(mesh):
    return jax.shard_map(
        local,
        mesh=mesh,
        in_specs=(
            P("section", "fsdp", None, None),
            P("section", "fsdp"),
            P("section", "fsdp", None),
            P(),
            P("section", None, None),
            P("section", None),
            P("fsdp"),
            P(None, "fsdp"),
        ),
        out_specs=(P("section"), P("section", "fsdp", None, None), P(None, "fsdp"), P("fsdp")),
        check_vma=False,
    )
```

```python
import jax
import jax.numpy as jnp
from jax import lax
from jax.experimental import pallas as pl
from jax.experimental.pallas import tpu as pltpu
from jax.sharding import PartitionSpec as P

D = 4096
BLOCK = 128
U = 8
K = 4
LEN = 256
SEQ_DEV = 3


eps = 1e-05
loss_scale = 256.0

MESH = pl.DeviceIdType.MESH
VMEM = pl.BlockSpec(memory_space=pltpu.VMEM)
SMEM = pl.BlockSpec(memory_space=pltpu.SMEM)
ANY = pl.BlockSpec(memory_space=pl.ANY)
bf16, f32 = jnp.bfloat16, jnp.float32


def greet(others):
    barrier = pltpu.get_barrier_semaphore()
    for device in others:
        pl.semaphore_signal(barrier, inc=1, device_id=device, device_id_type=MESH)
    pl.semaphore_wait(barrier, len(others))


def remote(src, dst, send, recv, device):
    return pltpu.make_async_remote_copy(
        src_ref=src,
        dst_ref=dst,
        send_sem=send,
        recv_sem=recv,
        device_id=device,
        device_id_type=MESH,
    )


def pick(hits, rows):
    return jnp.dot(hits, rows, precision=lax.Precision.HIGHEST, preferred_element_type=f32)


def collect_kernel(ids_ref, head_hbm, out_ref, sems):
    copies = []
    for u in range(U):
        start = pl.multiple_of(ids_ref[u] * BLOCK, BLOCK)
        copies.append(
            pltpu.make_async_copy(
                head_hbm.at[pl.ds(start, BLOCK)],
                out_ref.at[pl.ds(u * BLOCK, BLOCK)],
                sems.at[u],
            )
        )
    for copy in copies:
        copy.start()
    for copy in copies:
        copy.wait()


def collect_rows(ids, head):
    return pl.pallas_call(
        collect_kernel,
        name="collect_rows",
        out_shape=jax.ShapeDtypeStruct((U * BLOCK, head.shape[1]), head.dtype),
        in_specs=[SMEM, ANY],
        out_specs=VMEM,
        scratch_shapes=[pltpu.SemaphoreType.DMA((U,))],
    )(ids, head)


ZA, YA, XA, MA, ML, ZC, YC, MC = 0, 1, 2, 4, 6, 8, 9, 10
GATHER_GROUPS = 12


def whole_kernel(
    n, piece_hbm, gain_ref, token_hbm, lens_ref, slots_ref, triple_ref, teacher_ref,
    loss_out, grad_hbm, head_out, gain_out,
    token_ref, normed_ref, window, logits, inv_ref, weight_ref, gains, own_group, got_group,
    pool_ref, held, grad_ref, loss_ref, gl, turned,
    mpart, opart, got_mate, sum_x, got_x, sum_yc, got_yc, sum_ya, got_ya,
    sum_zc, got_zc, sum_za, got_za, total_a, total_c, dots_ref, final_a, final_c, got_a, got_c,
    product, gain_row, gain_own, got_gain, gain_sum, got_sum,
    token_sem, own_sem, store_sem, wsend, wrecv, gsend, grecv, qsend, qrecv, psend, precv,
    msend, mrecv, rsend, rrecv, osend, orecv, tsend, trecv, ssend, srecv,
):
    s, f = lax.axis_index("section"), lax.axis_index("fsdp")
    core = lax.rem(s, 2)
    mate = s + 1 - 2 * core
    across = lax.rem(s + 2, 4)
    diagonal = lax.rem(mate + 2, 4)
    lines = n // 2
    a, b = lax.div(f, 2), lax.rem(f, 2)
    terms, columns = piece_hbm.shape
    tall, width = token_ref.shape
    half_terms = terms // 2
    peers = [(s, lax.rem(f + d, n)) for d in range(1, n)]
    sections = [(lax.rem(s + d, 4), f) for d in range(1, 4)]
    y_side = (s, 2 * a + 1 - b)
    own = pltpu.make_async_copy(piece_hbm, window.at[f], own_sem)
    own.start()
    tokens = pltpu.make_async_copy(token_hbm, token_ref, token_sem)
    tokens.start()
    greet(peers + sections)
    sent = []

    def push(src, dst, send, recv, device, valid=None):
        copy = remote(src, dst, send, recv, device)
        if valid is None:
            copy.start()
        else:
            pl.when(valid)(copy.start)
        sent.append((copy, valid))

    def arrive(spot, send, recv):
        remote(spot, spot, send, recv, (mate, f)).wait_recv()

    part_a, part_c = terms * 3 // 16, terms // 8
    first_c = 4 * part_a

    def rows_a(q):
        return pl.ds(pl.multiple_of(q * part_a, 16), part_a)

    def rows_c(c):
        return pl.ds(pl.multiple_of(first_c + c * part_c, 16), part_c)

    def wpush(src, g, rows, group, q, device, valid=None):
        push(src, window.at[g, rows], wsend.at[group, q], wrecv.at[group, q], device, valid)

    def warrive(g, rows, group, q):
        spot = window.at[g, rows]
        arrive(spot, wsend.at[group, q], wrecv.at[group, q])
        return spot

    paired = jnp.minimum(a, lines - 1 - a)
    line, lower = [a], [0]
    for d in range(1, lines):
        below = jnp.where(d <= 2 * paired, d % 2, jnp.where(2 * a > lines - 1, 1, 0))
        distance = jnp.where(d <= 2 * paired, (d + 1) // 2, d - paired)
        line.append(a + (1 - 2 * below) * distance)
        lower.append(below)

    def name(d, half):
        return 2 * line[d] + (1 - b if half else b)

    def step_to(place):
        valid = (place >= 0) & (place < lines)
        return (s, 2 * lax.rem(place + lines, lines) + b), valid

    mine_a, mine_c = rows_a(s), rows_c(core)

    def begin(mine, group_z, group_y):
        src = window.at[f, mine]
        for place in (a - 1, a + 1):
            device, valid = step_to(place)
            wpush(src, f, mine, group_z, a, device, valid)
        wpush(src, f, mine, group_y, a, y_side)

    own.wait()
    begin(mine_a, ZA, YA)
    for k in range(columns // BLOCK):
        gains[f, :, k * BLOCK : (k + 1) * BLOCK] = gain_ref[k : k + 1, :].astype(f32)
    for d in range(1, n):
        push(gains.at[f], gains.at[f], gsend.at[d], grecv.at[d], peers[d - 1])
    own_group[...] = jnp.zeros_like(own_group)
    trips = teacher_ref.shape[1]
    for k in range(3):
        own_group[k : k + 1, :trips] = triple_ref[k].astype(f32)
    own_group[3:4, :trips] = teacher_ref[...]
    push(own_group, got_group, qsend.at[0], qrecv.at[0], sections[2])

    def relay(d, half, mine, group_z, group_y, group_m):
        g, q = name(d, half), line[d]
        spot = warrive(g, mine, group_y if half else group_z, q)
        if not half:
            device, valid = step_to(a + 2 * lower[d] - 1)
            wpush(spot, g, mine, group_z, q, device, valid)
            wpush(spot, g, mine, group_y, q, y_side)
        if group_m == MA:
            wpush(spot, g, mine, XA + half, q, (across, f))
        wpush(spot, g, mine, group_m + half, q, (mate, f))

    def relay_a(d, half):
        relay(d, half, mine_a, ZA, YA, MA)

    def relay_c(d, half):
        relay(d, half, mine_c, ZC, YC, MC)

    def relay_x(d, half):
        g, q = name(d, half), line[d]
        spot = warrive(g, rows_a(across), XA + half, q)
        wpush(spot, g, rows_a(across), ML + half, q, (mate, f))

    def rows_of(i):
        return pl.ds(pl.multiple_of(i * LEN, LEN), LEN)

    def cols_of(g):
        return pl.ds(pl.multiple_of(g * columns, columns), columns)

    def measure_block(i, carry):
        squares = jnp.zeros((LEN, 1), f32)
        for g in range(n):
            wide = token_ref[rows_of(i), g * columns : (g + 1) * columns].astype(f32)
            squares = squares + jnp.sum(wide * wide, axis=1, keepdims=True)
        inv_ref[rows_of(i), :] = lax.rsqrt(squares / width + eps)
        count = lens_ref[0, i]
        inside = lax.broadcasted_iota(jnp.int32, (LEN, BLOCK), 0) < count
        weight_ref[rows_of(i), :] = jnp.where(inside, 1.0, 0.0) / count.astype(f32)
        return carry

    def norm_block(i, carry):
        inv = inv_ref[rows_of(i), :]
        for g in range(n):
            cols = slice(g * columns, (g + 1) * columns)
            wide = token_ref[rows_of(i), cols].astype(f32)
            normed_ref[rows_of(i), cols] = (wide * inv * gains[g]).astype(bf16)
        return carry

    def add_logits(start, size, pieces, fresh=False):
        places = pl.ds(start if isinstance(start, int) else pl.multiple_of(start, BLOCK), size)
        value = None
        for g in pieces:
            part = lax.dot_general(
                normed_ref[:, cols_of(g)],
                window[g, places, :],
                (((1,), (1,)), ((), ())),
                preferred_element_type=f32,
            )
            value = part if value is None else value + part
        logits[:, places] = value if fresh else value + logits[:, places]

    chip = lax.div(s, 2)
    size_a, size_c = 2 * part_a, 2 * part_c

    def logits_of(pieces, start, size, rows, group):
        for d, half in pieces:
            warrive(name(d, half), rows, group + half, line[d])
        add_logits(start, size, [name(d, half) for d, half in pieces])

    def logits_a(*pieces):
        logits_of(pieces, chip * size_a, size_a, rows_a(mate), MA)

    def logits_c(*pieces):
        logits_of(pieces, first_c, size_c, rows_c(1 - core), MC)

    def logits_x(*pieces):
        logits_of(pieces, (1 - chip) * size_a, size_a, rows_a(diagonal), ML)

    def chosen(i, u):
        count = jnp.where(slots_ref[i, 0, 0] == u, 1.0, 0.0)
        for k in range(1, K):
            count = count + jnp.where(slots_ref[i, 0, k] == u, 1.0, 0.0)
        return count

    def lanes(u):
        return pl.ds(pl.multiple_of(u * BLOCK, BLOCK), BLOCK)

    step = 64

    def pool_blocks(first, count):
        def tile(index, carry):
            u, i = first + lax.div(index, SEQ_DEV), lax.rem(index, SEQ_DEV)
            total = jnp.zeros((1, BLOCK), f32)
            for k in range(LEN // step):
                rows = pl.ds(pl.multiple_of(i * LEN + k * step, step), step)
                x = logits[rows, lanes(u)]
                weight = weight_ref[rows, :]
                e = jnp.exp(-jnp.abs(x))
                smooth = jnp.maximum(x, 0.0) + jnp.log1p(e)
                total = total + jnp.sum(weight * jnp.log1p(smooth), axis=0, keepdims=True)
                top = jnp.where(x >= 0.0, 1.0, e)
                logits[rows, lanes(u)] = weight * top / ((1.0 + e) * (1.0 + smooth))
            pool_ref[pl.ds(i * U + u, 1), :] = total * chosen(i, u)
            return carry

        lax.fori_loop(0, count * SEQ_DEV, tile, 0)

    tokens.wait()
    lax.fori_loop(0, SEQ_DEV, measure_block, 0)
    relay_a(0, 1)
    relay_a(1, 0)
    for k in range(1, n):
        arrive(gains.at[lax.rem(f - k + n, n)], gsend.at[k], grecv.at[k])
    for d in range(2, lines):
        norm_block(d - 2, 0) if d < 2 + SEQ_DEV else None
        relay_a(d, 0)
        relay_a(d - 1, 1)
    begin(mine_c, ZC, YC)
    for i in range(lines - 2, SEQ_DEV):
        norm_block(i, 0)
    relay_a(lines - 1, 1)
    for j in range(2):
        add_logits(j * half_terms, half_terms, [f], fresh=True)
    order = [(0, 1), (1, 0)]
    for d in range(2, lines):
        order += [(d, 0), (d - 1, 1)]
    order.append((lines - 1, 1))
    groups = [order[i : i + 4] for i in range(0, len(order), 4)]
    for i, pieces in enumerate(groups):
        for piece in order[2 * i : 2 * i + 2]:
            relay_c(*piece)
        logits_a(*pieces)
    for piece in order[2 * len(groups) : -1]:
        relay_c(*piece)
    pool_blocks(chip * size_a // BLOCK, size_a // BLOCK)
    for piece in groups[0]:
        relay_x(*piece)
    relay_c(*order[-1])
    for i, pieces in enumerate(groups):
        logits_c(*pieces)
        if i > 0:
            for piece in groups[i][:-1] if i == len(groups) - 1 else groups[i]:
                relay_x(*piece)
        if i < len(groups) - 1:
            logits_x(*pieces)
    pool_blocks(first_c // BLOCK, size_c // BLOCK)
    relay_x(*order[-1])
    logits_x(*groups[-1])
    pool_blocks((1 - chip) * size_a // BLOCK, size_a // BLOCK)

    own_rows = SEQ_DEV * U
    for d in range(1, n):
        push(pool_ref, held.at[f], psend.at[d], precv.at[d], peers[d - 1])
    held[f] = pool_ref[...]
    arrive(got_group, qsend.at[0], qrecv.at[0])
    lifted = trips * U
    at = lax.broadcasted_iota(jnp.int32, (lifted, BLOCK), 0)
    ours = lax.broadcasted_iota(jnp.int32, (lifted, BLOCK), 1) == lax.div(at, U)
    group = [
        jnp.sum(jnp.where(ours, got_group[k : k + 1, :], 0.0), axis=1, keepdims=True)
        for k in range(4)
    ]
    within = lax.rem(lax.broadcasted_iota(jnp.int32, (lifted, 1), 0), U).astype(f32)
    aims = [group[k] * U + within for k in range(3)]
    names = lax.broadcasted_iota(jnp.int32, (lifted, n * own_rows), 1).astype(f32)
    hits = [jnp.where(names == aims[k], 1.0, 0.0) for k in range(3)]
    own_names = lax.broadcasted_iota(jnp.int32, (lifted, BLOCK), 1)
    own_at = jnp.where(own_names < own_rows, own_names + f * own_rows, -1).astype(f32)
    own_hits = [jnp.where(own_at == aims[k], 1.0, 0.0) for k in range(3)]
    triple = lambda dim: lax.div(lax.broadcasted_iota(jnp.int32, (lifted, lifted), dim), U)
    same = jnp.where(triple(0) == triple(1), 1.0, 0.0)
    for d in range(1, n):
        arrive(held.at[lax.rem(f - d + n, n)], psend.at[d], precv.at[d])
    rows = held[...].reshape(n * own_rows, BLOCK)
    query = pick(hits[0], rows)
    gap = pick(hits[1] - hits[2], rows)
    margin = jnp.sum(pick(same, query * gap), axis=1, keepdims=True)
    deviation = margin - group[3]
    loss = jnp.sum(deviation * deviation, axis=0, keepdims=True) / (trips * U)
    loss_ref[...] = jnp.broadcast_to(loss, loss_ref.shape)
    push(loss_ref, loss_out, qsend.at[1], qrecv.at[1], sections[0])
    grad_margin = loss_scale * 2.0 * deviation / trips
    back = (((0,), (0,)), ((), ()))
    grad = lax.dot_general(
        own_hits[0], grad_margin * gap, back,
        precision=lax.Precision.HIGHEST, preferred_element_type=f32,
    ) + lax.dot_general(
        own_hits[1] - own_hits[2], grad_margin * query, back,
        precision=lax.Precision.HIGHEST, preferred_element_type=f32,
    )
    grad_ref[...] = grad[:own_rows]

    def blocks_of(side_x, side_s, c):
        return [side_x, side_s, 4 + 2 * c, 5 + 2 * c]

    lists = [blocks_of(diagonal, mate, 1 - core), blocks_of(across, s, core)]

    def turn_blocks(places):
        for side in range(2):
            for p in places:
                u = lists[side][p]

                def turn(i, carry, u=u, p=p, side=side):
                    row = grad_ref[pl.ds(i * U + u, 1), :] * chosen(i, u)
                    value = logits[rows_of(i), lanes(u)] * row
                    gl[rows_of(i), lanes(u)] = value.astype(bf16)
                    turned[side, p * BLOCK : (p + 1) * BLOCK, rows_of(i)] = value.T.astype(bf16)
                    return carry

                lax.fori_loop(0, SEQ_DEV, turn, 0)

    chunk = line[:0:-1] + [a]
    rising = [1 - x for x in lower[:0:-1]]
    tile = 2 * columns if 2 * columns < 1024 else 1024
    def multiply(side, d, rows, out):
        def strip(j, carry):
            spot = pl.ds(pl.multiple_of(j * tile, tile), tile)
            source = pl.ds(pl.multiple_of(chunk[d] * 2 * columns + j * tile, tile), tile)
            out[d, rows, spot] = jnp.dot(
                turned[side, rows, :], normed_ref[:, source], preferred_element_type=f32
            ).astype(bf16)
            return carry

        lax.fori_loop(0, 2 * columns // tile, strip, 0)

    def to_mate(d, rows, kind):
        multiply(0, d, rows, mpart)
        push(
            mpart.at[d, rows], got_mate.at[d, rows],
            msend.at[kind, d], mrecv.at[kind, d], (mate, f),
        )

    def from_mate(d, rows, kind):
        arrive(got_mate.at[d, rows], msend.at[kind, d], mrecv.at[kind, d])

    def half(h):
        return pl.ds(pl.multiple_of(h * columns, columns), columns)

    r_x, r_a, r_c = slice(0, BLOCK), slice(BLOCK, 2 * BLOCK), slice(2 * BLOCK, 4 * BLOCK)
    RX, RYC, RYA, RZC, RZA = range(5)

    def rpush(src, dst, group, d, device):
        push(src, dst, rsend.at[group, d], rrecv.at[group, d], device)

    def rarrive(spot, group, d):
        arrive(spot, rsend.at[group, d], rrecv.at[group, d])

    def both(d, rows, cols):
        return opart[d, rows, cols].astype(f32) + got_mate[d, rows, cols].astype(f32)

    def stage_x(d):
        from_mate(d, r_x, 0)
        sum_x[d] = both(d, r_x, slice(None)).astype(bf16)
        rpush(sum_x.at[d], got_x.at[d], RX, d, (across, f))

    def stage_c(d):
        from_mate(d, r_c, 2)
        sum_yc[d] = both(d, r_c, half(1 - b)).astype(bf16)

    def push_c(d):
        rpush(sum_yc.at[d], got_yc.at[d], RYC, d, y_side)

    def await_c(d):
        rarrive(got_yc.at[d], RYC, d)

    def stage_y(d):
        from_mate(d, r_a, 1)
        rarrive(got_x.at[d], RX, d)
        value = both(d, r_a, half(1 - b)) + got_x[d, :, half(1 - b)].astype(f32)
        sum_ya[d] = value.astype(bf16)
        rpush(sum_ya.at[d], got_ya.at[d], RYA, d, y_side)

    def along_z(d, value, out, got, group):
        q, way = chunk[d], 2 * rising[d] - 1
        before = a - way
        comes = (before >= 0) & (before < lines)

        @pl.when(comes)
        def _():
            rarrive(got.at[q], group, q)
            out[d] = (value + got[q].astype(f32)).astype(bf16)

        @pl.when(jnp.logical_not(comes))
        def _():
            out[d] = value.astype(bf16)

        last = jnp.where(a + way == q, 1 - rising[d], 0)
        slot = q + last * (lines - q)
        device = (s, 2 * (a + way) + b)
        push_on = remote(out.at[d], got.at[slot], rsend.at[group, d], rrecv.at[group, slot], device)
        push_on.start()

    def end_z(got, total, group):
        for valid, slot in ((a > 0, a), (a < lines - 1, lines)):

            @pl.when(valid)
            def _(slot=slot):
                rarrive(got.at[slot], group, slot)
                total[...] += got[slot].astype(f32)

    def stage_zc(d):
        value = both(d, r_c, half(b)) + got_yc[d].astype(f32)
        if d == lines - 1:
            total_c[...] = value
        else:
            along_z(d, value, sum_zc, got_zc, RZC)

    def await_a(d):
        rarrive(got_ya.at[d], RYA, d)

    def stage_za(d):
        value = both(d, r_a, half(b)) + got_x[d, :, half(b)].astype(f32) + got_ya[d].astype(f32)
        if d == lines - 1:
            total_a[...] = value
        else:
            along_z(d, value, sum_za, got_za, RZA)

    def store(i):
        spot = pl.ds(i * LEN, LEN)
        return pltpu.make_async_copy(token_ref.at[spot], grad_hbm.at[spot], store_sem.at[i])

    def token_strips(i, first, count):
        spot = slice(i * LEN, (i + 1) * LEN)
        inv = inv_ref[spot, :]

        def strip(j, dots):
            for g in (first + 2 * j, first + 2 * j + 1):
                value = jnp.dot(gl[spot, :], window[g], preferred_element_type=f32)
                wide = token_ref[spot, cols_of(g)].astype(f32)
                row = jnp.sum(value * wide * inv, axis=0, keepdims=True)
                gain_row[g] = row if i == 0 else gain_row[g] + row
                scaled = value * gains[g]
                product[:, cols_of(g)] = scaled
                dots = dots + jnp.sum(scaled * wide, axis=1, keepdims=True)
            return dots

        start = dots_ref[...] if first else jnp.zeros((LEN, 1), f32)
        dots_ref[...] = lax.fori_loop(0, count // 2, strip, start)

    def token_finish(i):
        spot = slice(i * LEN, (i + 1) * LEN)
        inv = inv_ref[spot, :]
        factor = inv * inv * inv * (dots_ref[...] / width)

        def finish(g, carry):
            wide = token_ref[spot, cols_of(g)].astype(f32)
            token_ref[spot, cols_of(g)] = (inv * product[:, cols_of(g)] - wide * factor).astype(bf16)
            return carry

        lax.fori_loop(0, n, finish, 0)
        store(i).start()

    def to_gain_owners():
        for d in range(1, n):
            device = peers[d - 1]
            push(gain_row.at[device[1]], got_gain.at[d], tsend.at[d], trecv.at[d], device)

    turn_blocks((2, 3))
    to_mate(0, r_c, 2)
    multiply(1, 0, r_c, opart)
    turn_blocks((0,))
    stage_c(0)
    push_c(0)
    for d in range(lines):
        to_mate(d, r_x, 0)
    for d in range(lines):
        multiply(1, d, r_x, opart)
        stage_x(d)
    for d in range(1, lines):
        to_mate(d, r_c, 2)
        multiply(1, d, r_c, opart)
        stage_c(d)
        if d == 1:
            push_c(1)
            turn_blocks((1,))
            for k in range(lines):
                to_mate(k, r_a, 1)
                multiply(1, k, r_a, opart)
    over_y = [("c", 0)]
    for d in range(1, lines - 1):
        over_y += [("c", d), ("a", d - 1)]
    over_y += [("a", lines - 2), ("c", lines - 1), ("a", lines - 1)]
    begin_y = {"c": push_c, "a": stage_y}
    await_y = {"c": await_c, "a": await_a}
    next_z = {"c": stage_zc, "a": stage_za}
    edge = (a == 0) | (a == lines - 1)

    def pass_on(k, where):
        kind, d = over_y[k]

        @pl.when(where)
        def _():
            next_z[kind](d)

    for out, got, group in ((sum_zc, got_zc, RZC), (sum_za, got_za, RZA)):
        for d in range(lines - 1):
            whole = remote(out.at[d], got.at[0], rsend.at[group, d], rrecv.at[group, 0], (mate, f))
            sent.append((whole, None))

    beside = {
        2: [lambda: token_strips(0, 0, lines)],
        3: [lambda: token_strips(0, lines, lines), lambda: token_finish(0)],
        4: [lambda: token_strips(1, 0, lines)],
        5: [lambda: token_strips(1, lines, lines), lambda: token_finish(1)],
        6: [lambda: token_strips(2, 0, lines)],
        7: [lambda: token_strips(2, lines, lines), lambda: token_finish(2), to_gain_owners],
    }
    for k in range(2, len(over_y)):
        kind, d = over_y[k - 2]
        await_y[kind](d)
        begin_y[over_y[k][0]](over_y[k][1])
        pass_on(k - 2, edge)
        if k > 2:
            pass_on(k - 3, jnp.logical_not(edge))
        for work in beside.get(k, []):
            work()
    pass_on(len(over_y) - 3, jnp.logical_not(edge))
    await_c(lines - 1)
    stage_zc(lines - 1)
    end_z(got_zc, total_c, RZC)
    final_c[...] = total_c[...].astype(bf16)
    push(final_c, got_c, osend.at[0], orecv.at[0], (across, f))
    total = gain_row[f]
    for d in range(1, n):
        arrive(got_gain.at[d], tsend.at[d], trecv.at[d])
        total = total + got_gain[d]
    gain_sum[...] = total
    for d in range(1, 4):
        push(gain_sum, got_sum.at[d], ssend.at[d], srecv.at[d], sections[d - 1])
    await_a(lines - 1)
    stage_za(lines - 1)
    end_z(got_za, total_a, RZA)
    final_a[...] = total_a[...].astype(bf16)
    push(final_a, got_a.at[0], osend.at[1], orecv.at[1], (across, f))
    push(final_a, got_a.at[1], osend.at[2], orecv.at[2], (mate, f))

    def band(u, count=1):
        return pl.ds(pl.multiple_of(u * BLOCK, BLOCK), count * BLOCK)

    head_out[band(s), :] = final_a[...].astype(f32)
    arrive(got_c, osend.at[0], orecv.at[0])
    spot_c = head_out.at[band(4 + 2 * core, 2)]
    spot_c[...] = final_c[...].astype(f32) + got_c[...].astype(f32)
    push(spot_c, spot_c, osend.at[3], orecv.at[3], (mate, f))
    for d in range(1, 4):
        arrive(got_sum.at[d], ssend.at[d], srecv.at[d])
    gain_out[...] = gain_sum[...] + got_sum[1] + got_sum[2] + got_sum[3]
    arrive(got_a.at[1], osend.at[2], orecv.at[2])
    head_out[band(mate), :] = got_a[1].astype(f32)
    arrive(got_a.at[0], osend.at[1], orecv.at[1])
    push(got_a.at[0], got_a.at[2], osend.at[4], orecv.at[4], (mate, f))
    head_out[band(across), :] = got_a[0].astype(f32)
    arrive(head_out.at[band(6 - 2 * core, 2)], osend.at[3], orecv.at[3])
    arrive(got_a.at[2], osend.at[4], orecv.at[4])
    head_out[band(diagonal), :] = got_a[2].astype(f32)
    arrive(loss_out, qsend.at[1], qrecv.at[1])
    for i in range(SEQ_DEV):
        store(i).wait()
    for copy, valid in sent:
        if valid is None:
            copy.wait_send()
        else:
            pl.when(valid)(copy.wait_send)


def run_whole(piece, gain, tokens, lens, slots, triples, teacher, n):
    terms, columns = piece.shape
    tall, width = tokens.shape
    lines = n // 2
    own_rows = SEQ_DEV * U
    half_terms = terms // 2

    def vm(*shape, dtype=bf16):
        return pltpu.VMEM(shape, dtype)

    def pair(*shape):
        return [pltpu.SemaphoreType.DMA(shape)] * 2

    scratch = [
        vm(tall, width), vm(tall, width), vm(n, terms, columns), vm(tall, terms, dtype=f32),
        vm(tall, 1, dtype=f32), vm(tall, BLOCK, dtype=f32), vm(n, 1, columns, dtype=f32),
        vm(8, BLOCK, dtype=f32), vm(8, BLOCK, dtype=f32),
        vm(own_rows, BLOCK, dtype=f32), vm(n, own_rows, BLOCK, dtype=f32),
        vm(own_rows, BLOCK, dtype=f32), vm(1, 128, dtype=f32),
        vm(tall, terms), vm(2, half_terms, tall),
        vm(lines, half_terms, 2 * columns), vm(lines, half_terms, 2 * columns),
        vm(lines, half_terms, 2 * columns),
        vm(lines, BLOCK, 2 * columns), vm(lines, BLOCK, 2 * columns),
        vm(lines, 2 * BLOCK, columns), vm(lines, 2 * BLOCK, columns),
        vm(lines, BLOCK, columns), vm(lines, BLOCK, columns),
        vm(lines, 2 * BLOCK, columns), vm(lines + 1, 2 * BLOCK, columns),
        vm(lines, BLOCK, columns), vm(lines + 1, BLOCK, columns),
        vm(BLOCK, columns, dtype=f32), vm(2 * BLOCK, columns, dtype=f32), vm(LEN, 1, dtype=f32),
        vm(BLOCK, columns), vm(2 * BLOCK, columns),
        vm(3, BLOCK, columns), vm(2 * BLOCK, columns),
        vm(LEN, width, dtype=f32), vm(n, 1, columns, dtype=f32), vm(1, columns, dtype=f32),
        vm(n, 1, columns, dtype=f32), vm(1, columns, dtype=f32), vm(4, 1, columns, dtype=f32),
        pltpu.SemaphoreType.DMA, pltpu.SemaphoreType.DMA, pltpu.SemaphoreType.DMA((SEQ_DEV,)),
    ]
    scratch += pair(GATHER_GROUPS, lines) + pair(n) + pair(2) + pair(n)
    scratch += pair(3, lines) + pair(5, lines + 1) + pair(5) + pair(n) + pair(4)
    return pl.pallas_call(
        lambda *refs: whole_kernel(n, *refs),
        name="splade_step",
        out_shape=(
            jax.ShapeDtypeStruct((1, 128), f32),
            jax.ShapeDtypeStruct((tall, width), bf16),
            jax.ShapeDtypeStruct((terms, columns), f32),
            jax.ShapeDtypeStruct((1, columns), f32),
        ),
        in_specs=[ANY, VMEM, ANY, SMEM, SMEM, VMEM, VMEM],
        out_specs=(VMEM, ANY, VMEM, VMEM),
        scratch_shapes=scratch,
        compiler_params=pltpu.CompilerParams(
            collective_id=0, has_side_effects=True, vmem_limit_bytes=62 << 20
        ),
    )(piece, gain, tokens, lens, slots, triples, teacher)


def hand_kernel(cuts, *refs):
    count = len(cuts)
    ins, outs, held = refs[:count], refs[count : 2 * count], refs[2 * count : 3 * count]
    load_sem, store_sem = refs[3 * count :]
    loads, stores = [], []
    for src, dst, buffer, cut in zip(ins, outs, held, cuts):
        rows = src.shape[0] // cut
        for i in range(cut):
            spot, index = pl.ds(i * rows, rows), len(loads)
            loads.append(pltpu.make_async_copy(src.at[spot], buffer.at[spot], load_sem.at[index]))
            stores.append(pltpu.make_async_copy(buffer.at[spot], dst.at[spot], store_sem.at[index]))
    for load in loads:
        load.start()
    for load, store in zip(loads, stores):
        load.wait()
        store.start()
    for store in stores:
        store.wait()


def hand_out(*arrays):
    cuts = [max(1, x.size * x.dtype.itemsize >> 20) for x in arrays]
    return pl.pallas_call(
        lambda *refs: hand_kernel(cuts, *refs),
        name="hand_out",
        out_shape=tuple(jax.ShapeDtypeStruct(x.shape, x.dtype) for x in arrays),
        in_specs=[ANY] * len(arrays),
        out_specs=(ANY,) * len(arrays),
        scratch_shapes=[pltpu.VMEM(x.shape, x.dtype) for x in arrays]
        + [pltpu.SemaphoreType.DMA((sum(cuts),))] * 2,
        compiler_params=pltpu.CompilerParams(vmem_limit_bytes=62 << 20),
    )(*arrays)


def local(produced, lengths, active, window_blocks, triplets, teacher, norm_gain, head):
    shards = lax.axis_size("fsdp")
    columns = head.shape[1]
    piece = collect_rows(window_blocks, head)
    gain = norm_gain.reshape(columns // BLOCK, BLOCK)
    tokens = produced.reshape(SEQ_DEV * LEN, D)
    results = run_whole(
        piece, gain, tokens, lengths, active.transpose(1, 0, 2),
        triplets.transpose(2, 0, 1), teacher, shards,
    )
    loss_row, grad_tokens, head_grad, gain_grad = hand_out(*results)
    return (
        loss_row[0, :1],
        grad_tokens.reshape(1, SEQ_DEV, LEN, D),
        head_grad,
        gain_grad.reshape(columns),
    )


def solution(mesh):
    return jax.shard_map(
        local,
        mesh=mesh,
        in_specs=(
            P("section", "fsdp", None, None),
            P("section", "fsdp"),
            P("section", "fsdp", None),
            P(),
            P("section", None, None),
            P("section", None),
            P("fsdp"),
            P(None, "fsdp"),
        ),
        out_specs=(P("section"), P("section", "fsdp", None, None), P(None, "fsdp"), P("fsdp")),
        check_vma=False,
    )
```

```python
import jax
import jax.numpy as jnp
from jax import lax
from jax.experimental import pallas as pl
from jax.experimental.pallas import tpu as pltpu
from jax.sharding import PartitionSpec as P

D = 4096
BLOCK = 128
U = 8
K = 4
LEN = 256
SEQ_DEV = 3


eps = 1e-05
loss_scale = 256.0

MESH = pl.DeviceIdType.MESH
VMEM = pl.BlockSpec(memory_space=pltpu.VMEM)
SMEM = pl.BlockSpec(memory_space=pltpu.SMEM)
ANY = pl.BlockSpec(memory_space=pl.ANY)
bf16, f32 = jnp.bfloat16, jnp.float32


def greet(others):
    barrier = pltpu.get_barrier_semaphore()
    for device in others:
        pl.semaphore_signal(barrier, inc=1, device_id=device, device_id_type=MESH)
    pl.semaphore_wait(barrier, len(others))


def remote(src, dst, send, recv, device):
    return pltpu.make_async_remote_copy(
        src_ref=src,
        dst_ref=dst,
        send_sem=send,
        recv_sem=recv,
        device_id=device,
        device_id_type=MESH,
    )


def pick(hits, rows):
    return jnp.dot(hits, rows, precision=lax.Precision.HIGHEST, preferred_element_type=f32)


def collect_kernel(ids_ref, head_hbm, out_ref, sems):
    copies = []
    for u in range(U):
        start = pl.multiple_of(ids_ref[u] * BLOCK, BLOCK)
        copies.append(
            pltpu.make_async_copy(
                head_hbm.at[pl.ds(start, BLOCK)],
                out_ref.at[pl.ds(u * BLOCK, BLOCK)],
                sems.at[u],
            )
        )
    for copy in copies:
        copy.start()
    for copy in copies:
        copy.wait()


def collect_rows(ids, head):
    return pl.pallas_call(
        collect_kernel,
        name="collect_rows",
        out_shape=jax.ShapeDtypeStruct((U * BLOCK, head.shape[1]), head.dtype),
        in_specs=[SMEM, ANY],
        out_specs=VMEM,
        scratch_shapes=[pltpu.SemaphoreType.DMA((U,))],
    )(ids, head)


ZA, YA, XA, MA, ML, ZC, YC, MC = 0, 1, 2, 4, 6, 8, 9, 10
GATHER_GROUPS = 12


def whole_kernel(
    n, piece_hbm, gain_ref, token_hbm, lens_ref, slots_ref, triple_ref, teacher_ref,
    loss_out, grad_hbm, head_out, gain_out,
    token_ref, normed_ref, window, logits, inv_ref, weight_ref, gains, own_group, got_group,
    pool_ref, held, grad_ref, loss_ref, gl, turned,
    mpart, opart, got_mate, sum_x, got_x, sum_yc, got_yc, sum_ya, got_ya,
    sum_zc, got_zc, sum_za, got_za, total_a, total_c, dots_ref, final_a, final_c, got_a, got_c,
    product, gain_row, gain_own, got_gain, gain_sum, got_sum,
    token_sem, own_sem, store_sem, wsend, wrecv, gsend, grecv, qsend, qrecv, psend, precv,
    msend, mrecv, rsend, rrecv, osend, orecv, tsend, trecv, ssend, srecv,
):
    s, f = lax.axis_index("section"), lax.axis_index("fsdp")
    core = lax.rem(s, 2)
    mate = s + 1 - 2 * core
    across = lax.rem(s + 2, 4)
    diagonal = lax.rem(mate + 2, 4)
    lines = n // 2
    a, b = lax.div(f, 2), lax.rem(f, 2)
    terms, columns = piece_hbm.shape
    tall, width = token_ref.shape
    half_terms = terms // 2
    peers = [(s, lax.rem(f + d, n)) for d in range(1, n)]
    sections = [(lax.rem(s + d, 4), f) for d in range(1, 4)]
    y_side = (s, 2 * a + 1 - b)
    own = pltpu.make_async_copy(piece_hbm, window.at[f], own_sem)
    own.start()
    tokens = pltpu.make_async_copy(token_hbm, token_ref, token_sem)
    tokens.start()
    greet(peers + sections)
    sent = []

    def push(src, dst, send, recv, device, valid=None):
        copy = remote(src, dst, send, recv, device)
        if valid is None:
            copy.start()
        else:
            pl.when(valid)(copy.start)
        sent.append((copy, valid))

    def arrive(spot, send, recv):
        remote(spot, spot, send, recv, (mate, f)).wait_recv()

    part_a, part_c = terms * 3 // 16, terms // 8
    first_c = 4 * part_a

    def rows_a(q):
        return pl.ds(pl.multiple_of(q * part_a, 16), part_a)

    def rows_c(c):
        return pl.ds(pl.multiple_of(first_c + c * part_c, 16), part_c)

    def wpush(src, g, rows, group, q, device, valid=None):
        push(src, window.at[g, rows], wsend.at[group, q], wrecv.at[group, q], device, valid)

    def warrive(g, rows, group, q):
        spot = window.at[g, rows]
        arrive(spot, wsend.at[group, q], wrecv.at[group, q])
        return spot

    paired = jnp.minimum(a, lines - 1 - a)
    line, lower = [a], [0]
    for d in range(1, lines):
        below = jnp.where(d <= 2 * paired, d % 2, jnp.where(2 * a > lines - 1, 1, 0))
        distance = jnp.where(d <= 2 * paired, (d + 1) // 2, d - paired)
        line.append(a + (1 - 2 * below) * distance)
        lower.append(below)

    def name(d, half):
        return 2 * line[d] + (1 - b if half else b)

    def step_to(place):
        valid = (place >= 0) & (place < lines)
        return (s, 2 * lax.rem(place + lines, lines) + b), valid

    mine_a, mine_c = rows_a(s), rows_c(core)

    def begin(mine, group_z, group_y):
        src = window.at[f, mine]
        for place in (a - 1, a + 1):
            device, valid = step_to(place)
            wpush(src, f, mine, group_z, a, device, valid)
        wpush(src, f, mine, group_y, a, y_side)

    own.wait()
    begin(mine_a, ZA, YA)
    for k in range(columns // BLOCK):
        gains[f, :, k * BLOCK : (k + 1) * BLOCK] = gain_ref[k : k + 1, :].astype(f32)
    for d in range(1, n):
        push(gains.at[f], gains.at[f], gsend.at[d], grecv.at[d], peers[d - 1])
    own_group[...] = jnp.zeros_like(own_group)
    trips = teacher_ref.shape[1]
    for k in range(3):
        own_group[k : k + 1, :trips] = triple_ref[k].astype(f32)
    own_group[3:4, :trips] = teacher_ref[...]
    push(own_group, got_group, qsend.at[0], qrecv.at[0], sections[2])

    def relay(d, half, mine, group_z, group_y, group_m):
        g, q = name(d, half), line[d]
        spot = warrive(g, mine, group_y if half else group_z, q)
        if not half:
            device, valid = step_to(a + 2 * lower[d] - 1)
            wpush(spot, g, mine, group_z, q, device, valid)
            wpush(spot, g, mine, group_y, q, y_side)
        if group_m == MA:
            wpush(spot, g, mine, XA + half, q, (across, f))
        wpush(spot, g, mine, group_m + half, q, (mate, f))

    def relay_a(d, half):
        relay(d, half, mine_a, ZA, YA, MA)

    def relay_c(d, half):
        relay(d, half, mine_c, ZC, YC, MC)

    def relay_x(d, half):
        g, q = name(d, half), line[d]
        spot = warrive(g, rows_a(across), XA + half, q)
        wpush(spot, g, rows_a(across), ML + half, q, (mate, f))

    def rows_of(i):
        return pl.ds(pl.multiple_of(i * LEN, LEN), LEN)

    def cols_of(g):
        return pl.ds(pl.multiple_of(g * columns, columns), columns)

    def measure_block(i, carry):
        squares = jnp.zeros((LEN, 1), f32)
        for g in range(n):
            wide = token_ref[rows_of(i), g * columns : (g + 1) * columns].astype(f32)
            squares = squares + jnp.sum(wide * wide, axis=1, keepdims=True)
        inv_ref[rows_of(i), :] = lax.rsqrt(squares / width + eps)
        count = lens_ref[0, i]
        inside = lax.broadcasted_iota(jnp.int32, (LEN, BLOCK), 0) < count
        weight_ref[rows_of(i), :] = jnp.where(inside, 1.0, 0.0) / count.astype(f32)
        return carry

    def norm_block(i, carry):
        inv = inv_ref[rows_of(i), :]
        for g in range(n):
            cols = slice(g * columns, (g + 1) * columns)
            wide = token_ref[rows_of(i), cols].astype(f32)
            normed_ref[rows_of(i), cols] = (wide * inv * gains[g]).astype(bf16)
        return carry

    def add_logits(start, size, pieces, fresh=False):
        places = pl.ds(start if isinstance(start, int) else pl.multiple_of(start, BLOCK), size)
        value = None
        for g in pieces:
            part = lax.dot_general(
                normed_ref[:, cols_of(g)],
                window[g, places, :],
                (((1,), (1,)), ((), ())),
                preferred_element_type=f32,
            )
            value = part if value is None else value + part
        logits[:, places] = value if fresh else value + logits[:, places]

    chip = lax.div(s, 2)
    size_a, size_c = 2 * part_a, 2 * part_c

    def logits_of(pieces, start, size, rows, group):
        for d, half in pieces:
            warrive(name(d, half), rows, group + half, line[d])
        add_logits(start, size, [name(d, half) for d, half in pieces])

    def logits_a(*pieces):
        logits_of(pieces, chip * size_a, size_a, rows_a(mate), MA)

    def logits_c(*pieces):
        logits_of(pieces, first_c, size_c, rows_c(1 - core), MC)

    def logits_x(*pieces):
        logits_of(pieces, (1 - chip) * size_a, size_a, rows_a(diagonal), ML)

    def chosen(i, u):
        count = jnp.where(slots_ref[i, 0, 0] == u, 1.0, 0.0)
        for k in range(1, K):
            count = count + jnp.where(slots_ref[i, 0, k] == u, 1.0, 0.0)
        return count

    def lanes(u):
        return pl.ds(pl.multiple_of(u * BLOCK, BLOCK), BLOCK)

    step = 64

    def pool_blocks(first, count):
        def tile(index, carry):
            u, i = first + lax.div(index, SEQ_DEV), lax.rem(index, SEQ_DEV)
            total = jnp.zeros((1, BLOCK), f32)
            for k in range(LEN // step):
                rows = pl.ds(pl.multiple_of(i * LEN + k * step, step), step)
                x = logits[rows, lanes(u)]
                weight = weight_ref[rows, :]
                e = jnp.exp(-jnp.abs(x))
                smooth = jnp.maximum(x, 0.0) + jnp.log1p(e)
                total = total + jnp.sum(weight * jnp.log1p(smooth), axis=0, keepdims=True)
                top = jnp.where(x >= 0.0, 1.0, e)
                logits[rows, lanes(u)] = weight * top / ((1.0 + e) * (1.0 + smooth))
            pool_ref[pl.ds(i * U + u, 1), :] = total * chosen(i, u)
            return carry

        lax.fori_loop(0, count * SEQ_DEV, tile, 0)

    tokens.wait()
    lax.fori_loop(0, SEQ_DEV, measure_block, 0)
    order = [(0, 1), (1, 0)]
    for d in range(2, lines):
        order += [(d, 0), (d - 1, 1)]
    order.append((lines - 1, 1))
    groups = [order[i : i + 4] for i in range(0, len(order), 4)]
    relay_a(0, 1)
    relay_a(1, 0)
    begin(mine_c, ZC, YC)
    for k in range(1, n):
        arrive(gains.at[lax.rem(f - k + n, n)], gsend.at[k], grecv.at[k])
    norm_block(0, 0)
    norm_block(1, 0)
    for d in range(2, lines):
        relay_a(d, 0)
        relay_a(d - 1, 1)
        if d == 2:
            norm_block(2, 0)
        relay_c(d - 1, 0)
        relay_c(d - 2, 1)
        if d == 2:
            for j in range(2):
                add_logits(j * half_terms, half_terms, [f], fresh=True)
    relay_a(lines - 1, 1)
    logits_a(*groups[0])
    relay_c(lines - 1, 0)
    relay_c(lines - 2, 1)
    for pieces in groups[1:]:
        logits_a(*pieces)
    pool_blocks(chip * size_a // BLOCK, size_a // BLOCK)
    for piece in groups[0]:
        relay_x(*piece)
    relay_c(*order[-1])
    for i, pieces in enumerate(groups):
        logits_c(*pieces)
        if i > 0:
            for piece in groups[i][:-1] if i == len(groups) - 1 else groups[i]:
                relay_x(*piece)
        if i < len(groups) - 1:
            logits_x(*pieces)
    pool_blocks(first_c // BLOCK, size_c // BLOCK)
    relay_x(*order[-1])
    logits_x(*groups[-1])
    pool_blocks((1 - chip) * size_a // BLOCK, size_a // BLOCK)

    own_rows = SEQ_DEV * U
    for d in range(1, n):
        push(pool_ref, held.at[f], psend.at[d], precv.at[d], peers[d - 1])
    held[f] = pool_ref[...]
    arrive(got_group, qsend.at[0], qrecv.at[0])
    lifted = trips * U
    at = lax.broadcasted_iota(jnp.int32, (lifted, BLOCK), 0)
    ours = lax.broadcasted_iota(jnp.int32, (lifted, BLOCK), 1) == lax.div(at, U)
    group = [
        jnp.sum(jnp.where(ours, got_group[k : k + 1, :], 0.0), axis=1, keepdims=True)
        for k in range(4)
    ]
    within = lax.rem(lax.broadcasted_iota(jnp.int32, (lifted, 1), 0), U).astype(f32)
    aims = [group[k] * U + within for k in range(3)]
    names = lax.broadcasted_iota(jnp.int32, (lifted, n * own_rows), 1).astype(f32)
    hits = [jnp.where(names == aims[k], 1.0, 0.0) for k in range(3)]
    own_names = lax.broadcasted_iota(jnp.int32, (lifted, BLOCK), 1)
    own_at = jnp.where(own_names < own_rows, own_names + f * own_rows, -1).astype(f32)
    own_hits = [jnp.where(own_at == aims[k], 1.0, 0.0) for k in range(3)]
    triple = lambda dim: lax.div(lax.broadcasted_iota(jnp.int32, (lifted, lifted), dim), U)
    same = jnp.where(triple(0) == triple(1), 1.0, 0.0)
    for d in range(1, n):
        arrive(held.at[lax.rem(f - d + n, n)], psend.at[d], precv.at[d])
    rows = held[...].reshape(n * own_rows, BLOCK)
    query = pick(hits[0], rows)
    gap = pick(hits[1] - hits[2], rows)
    margin = jnp.sum(pick(same, query * gap), axis=1, keepdims=True)
    deviation = margin - group[3]
    loss = jnp.sum(deviation * deviation, axis=0, keepdims=True) / (trips * U)
    loss_ref[...] = jnp.broadcast_to(loss, loss_ref.shape)
    push(loss_ref, loss_out, qsend.at[1], qrecv.at[1], sections[0])
    grad_margin = loss_scale * 2.0 * deviation / trips
    back = (((0,), (0,)), ((), ()))
    grad = lax.dot_general(
        own_hits[0], grad_margin * gap, back,
        precision=lax.Precision.HIGHEST, preferred_element_type=f32,
    ) + lax.dot_general(
        own_hits[1] - own_hits[2], grad_margin * query, back,
        precision=lax.Precision.HIGHEST, preferred_element_type=f32,
    )
    grad_ref[...] = grad[:own_rows]

    def blocks_of(side_x, side_s, c):
        return [side_x, side_s, 4 + 2 * c, 5 + 2 * c]

    lists = [blocks_of(diagonal, mate, 1 - core), blocks_of(across, s, core)]

    def turn_blocks(places):
        for side in range(2):
            for p in places:
                u = lists[side][p]

                def turn(i, carry, u=u, p=p, side=side):
                    row = grad_ref[pl.ds(i * U + u, 1), :] * chosen(i, u)
                    value = logits[rows_of(i), lanes(u)] * row
                    gl[rows_of(i), lanes(u)] = value.astype(bf16)
                    turned[side, p * BLOCK : (p + 1) * BLOCK, rows_of(i)] = value.T.astype(bf16)
                    return carry

                lax.fori_loop(0, SEQ_DEV, turn, 0)

    chunk = line[:0:-1] + [a]
    rising = [1 - x for x in lower[:0:-1]]
    tile = 2 * columns if 2 * columns < 1024 else 1024
    def multiply(side, d, rows, out):
        def strip(j, carry):
            spot = pl.ds(pl.multiple_of(j * tile, tile), tile)
            source = pl.ds(pl.multiple_of(chunk[d] * 2 * columns + j * tile, tile), tile)
            out[d, rows, spot] = jnp.dot(
                turned[side, rows, :], normed_ref[:, source], preferred_element_type=f32
            ).astype(bf16)
            return carry

        lax.fori_loop(0, 2 * columns // tile, strip, 0)

    def to_mate(d, rows, kind):
        multiply(0, d, rows, mpart)
        push(
            mpart.at[d, rows], got_mate.at[d, rows],
            msend.at[kind, d], mrecv.at[kind, d], (mate, f),
        )

    def from_mate(d, rows, kind):
        arrive(got_mate.at[d, rows], msend.at[kind, d], mrecv.at[kind, d])

    def half(h):
        return pl.ds(pl.multiple_of(h * columns, columns), columns)

    r_x, r_a, r_c = slice(0, BLOCK), slice(BLOCK, 2 * BLOCK), slice(2 * BLOCK, 4 * BLOCK)
    RX, RYC, RYA, RZC, RZA = range(5)

    def rpush(src, dst, group, d, device):
        push(src, dst, rsend.at[group, d], rrecv.at[group, d], device)

    def rarrive(spot, group, d):
        arrive(spot, rsend.at[group, d], rrecv.at[group, d])

    def both(d, rows, cols):
        return opart[d, rows, cols].astype(f32) + got_mate[d, rows, cols].astype(f32)

    def stage_x(d):
        from_mate(d, r_x, 0)
        sum_x[d] = both(d, r_x, slice(None)).astype(bf16)
        rpush(sum_x.at[d], got_x.at[d], RX, d, (across, f))

    def stage_c(d):
        from_mate(d, r_c, 2)
        sum_yc[d] = both(d, r_c, half(1 - b)).astype(bf16)

    def push_c(d):
        rpush(sum_yc.at[d], got_yc.at[d], RYC, d, y_side)

    def await_c(d):
        rarrive(got_yc.at[d], RYC, d)

    def stage_y(d):
        from_mate(d, r_a, 1)
        rarrive(got_x.at[d], RX, d)
        value = both(d, r_a, half(1 - b)) + got_x[d, :, half(1 - b)].astype(f32)
        sum_ya[d] = value.astype(bf16)
        rpush(sum_ya.at[d], got_ya.at[d], RYA, d, y_side)

    def along_z(d, value, out, got, group):
        q, way = chunk[d], 2 * rising[d] - 1
        before = a - way
        comes = (before >= 0) & (before < lines)

        @pl.when(comes)
        def _():
            rarrive(got.at[q], group, q)
            out[d] = (value + got[q].astype(f32)).astype(bf16)

        @pl.when(jnp.logical_not(comes))
        def _():
            out[d] = value.astype(bf16)

        last = jnp.where(a + way == q, 1 - rising[d], 0)
        slot = q + last * (lines - q)
        device = (s, 2 * (a + way) + b)
        push_on = remote(out.at[d], got.at[slot], rsend.at[group, d], rrecv.at[group, slot], device)
        push_on.start()

    def end_z(got, total, group):
        for valid, slot in ((a > 0, a), (a < lines - 1, lines)):

            @pl.when(valid)
            def _(slot=slot):
                rarrive(got.at[slot], group, slot)
                total[...] += got[slot].astype(f32)

    def stage_zc(d):
        value = both(d, r_c, half(b)) + got_yc[d].astype(f32)
        if d == lines - 1:
            total_c[...] = value
        else:
            along_z(d, value, sum_zc, got_zc, RZC)

    def await_a(d):
        rarrive(got_ya.at[d], RYA, d)

    def stage_za(d):
        value = both(d, r_a, half(b)) + got_x[d, :, half(b)].astype(f32) + got_ya[d].astype(f32)
        if d == lines - 1:
            total_a[...] = value
        else:
            along_z(d, value, sum_za, got_za, RZA)

    def store(i):
        spot = pl.ds(i * LEN, LEN)
        return pltpu.make_async_copy(token_ref.at[spot], grad_hbm.at[spot], store_sem.at[i])

    def token_strips(i, first, count):
        spot = slice(i * LEN, (i + 1) * LEN)
        inv = inv_ref[spot, :]

        def strip(j, dots):
            for g in (first + 2 * j, first + 2 * j + 1):
                value = jnp.dot(gl[spot, :], window[g], preferred_element_type=f32)
                wide = token_ref[spot, cols_of(g)].astype(f32)
                row = jnp.sum(value * wide * inv, axis=0, keepdims=True)
                gain_row[g] = row if i == 0 else gain_row[g] + row
                scaled = value * gains[g]
                product[:, cols_of(g)] = scaled
                dots = dots + jnp.sum(scaled * wide, axis=1, keepdims=True)
            return dots

        start = dots_ref[...] if first else jnp.zeros((LEN, 1), f32)
        dots_ref[...] = lax.fori_loop(0, count // 2, strip, start)

    def token_finish(i):
        spot = slice(i * LEN, (i + 1) * LEN)
        inv = inv_ref[spot, :]
        factor = inv * inv * inv * (dots_ref[...] / width)

        def finish(g, carry):
            wide = token_ref[spot, cols_of(g)].astype(f32)
            token_ref[spot, cols_of(g)] = (inv * product[:, cols_of(g)] - wide * factor).astype(bf16)
            return carry

        lax.fori_loop(0, n, finish, 0)
        store(i).start()

    def to_gain_owners():
        for d in range(1, n):
            device = peers[d - 1]
            push(gain_row.at[device[1]], got_gain.at[d], tsend.at[d], trecv.at[d], device)

    turn_blocks((2, 3))
    to_mate(0, r_c, 2)
    multiply(1, 0, r_c, opart)
    turn_blocks((0,))
    stage_c(0)
    push_c(0)
    for d in range(lines):
        to_mate(d, r_x, 0)
    for d in range(lines):
        multiply(1, d, r_x, opart)
        stage_x(d)
    def prepare(kind, d):
        rows = r_c if kind == "c" else r_a
        to_mate(d, rows, 2 if kind == "c" else 1)
        multiply(1, d, rows, opart)
        if kind == "c":
            stage_c(d)

    prepare("c", 1)
    push_c(1)
    turn_blocks((1,))
    prepare("a", 0)
    over_y = [("c", 0)]
    for d in range(1, lines - 1):
        over_y += [("c", d), ("a", d - 1)]
    over_y += [("a", lines - 2), ("c", lines - 1), ("a", lines - 1)]
    begin_y = {"c": push_c, "a": stage_y}
    await_y = {"c": await_c, "a": await_a}
    next_z = {"c": stage_zc, "a": stage_za}
    edge = (a == 0) | (a == lines - 1)

    def pass_on(k, where):
        kind, d = over_y[k]

        @pl.when(where)
        def _():
            next_z[kind](d)

    for out, got, group in ((sum_zc, got_zc, RZC), (sum_za, got_za, RZA)):
        for d in range(lines - 1):
            whole = remote(out.at[d], got.at[0], rsend.at[group, d], rrecv.at[group, 0], (mate, f))
            sent.append((whole, None))

    beside = {
        2: [lambda: token_strips(0, 0, lines)],
        3: [lambda: token_strips(0, lines, lines), lambda: token_finish(0)],
        4: [lambda: token_strips(1, 0, lines)],
        5: [lambda: token_strips(1, lines, lines), lambda: token_finish(1)],
        6: [lambda: token_strips(2, 0, lines)],
        7: [lambda: token_strips(2, lines, lines), lambda: token_finish(2), to_gain_owners],
    }
    for k in range(2, len(over_y)):
        kind, d = over_y[k - 2]
        await_y[kind](d)
        begin_y[over_y[k][0]](over_y[k][1])
        pass_on(k - 2, edge)
        if k > 2:
            pass_on(k - 3, jnp.logical_not(edge))
        if k + 1 < len(over_y):
            prepare(*over_y[k + 1])
        for work in beside.get(k, []):
            work()
    pass_on(len(over_y) - 3, jnp.logical_not(edge))
    await_c(lines - 1)
    stage_zc(lines - 1)
    end_z(got_zc, total_c, RZC)
    final_c[...] = total_c[...].astype(bf16)
    push(final_c, got_c, osend.at[0], orecv.at[0], (across, f))
    total = gain_row[f]
    for d in range(1, n):
        arrive(got_gain.at[d], tsend.at[d], trecv.at[d])
        total = total + got_gain[d]
    gain_sum[...] = total
    for d in range(1, 4):
        push(gain_sum, got_sum.at[d], ssend.at[d], srecv.at[d], sections[d - 1])
    await_a(lines - 1)
    stage_za(lines - 1)
    end_z(got_za, total_a, RZA)
    final_a[...] = total_a[...].astype(bf16)
    push(final_a, got_a.at[0], osend.at[1], orecv.at[1], (across, f))
    push(final_a, got_a.at[1], osend.at[2], orecv.at[2], (mate, f))

    def band(u, count=1):
        return pl.ds(pl.multiple_of(u * BLOCK, BLOCK), count * BLOCK)

    head_out[band(s), :] = final_a[...].astype(f32)
    arrive(got_c, osend.at[0], orecv.at[0])
    spot_c = head_out.at[band(4 + 2 * core, 2)]
    spot_c[...] = final_c[...].astype(f32) + got_c[...].astype(f32)
    push(spot_c, spot_c, osend.at[3], orecv.at[3], (mate, f))
    for d in range(1, 4):
        arrive(got_sum.at[d], ssend.at[d], srecv.at[d])
    gain_out[...] = gain_sum[...] + got_sum[1] + got_sum[2] + got_sum[3]
    arrive(got_a.at[1], osend.at[2], orecv.at[2])
    head_out[band(mate), :] = got_a[1].astype(f32)
    arrive(got_a.at[0], osend.at[1], orecv.at[1])
    push(got_a.at[0], got_a.at[2], osend.at[4], orecv.at[4], (mate, f))
    head_out[band(across), :] = got_a[0].astype(f32)
    arrive(head_out.at[band(6 - 2 * core, 2)], osend.at[3], orecv.at[3])
    arrive(got_a.at[2], osend.at[4], orecv.at[4])
    head_out[band(diagonal), :] = got_a[2].astype(f32)
    arrive(loss_out, qsend.at[1], qrecv.at[1])
    for i in range(SEQ_DEV):
        store(i).wait()
    for copy, valid in sent:
        if valid is None:
            copy.wait_send()
        else:
            pl.when(valid)(copy.wait_send)


def run_whole(piece, gain, tokens, lens, slots, triples, teacher, n):
    terms, columns = piece.shape
    tall, width = tokens.shape
    lines = n // 2
    own_rows = SEQ_DEV * U
    half_terms = terms // 2

    def vm(*shape, dtype=bf16):
        return pltpu.VMEM(shape, dtype)

    def pair(*shape):
        return [pltpu.SemaphoreType.DMA(shape)] * 2

    scratch = [
        vm(tall, width), vm(tall, width), vm(n, terms, columns), vm(tall, terms, dtype=f32),
        vm(tall, 1, dtype=f32), vm(tall, BLOCK, dtype=f32), vm(n, 1, columns, dtype=f32),
        vm(8, BLOCK, dtype=f32), vm(8, BLOCK, dtype=f32),
        vm(own_rows, BLOCK, dtype=f32), vm(n, own_rows, BLOCK, dtype=f32),
        vm(own_rows, BLOCK, dtype=f32), vm(1, 128, dtype=f32),
        vm(tall, terms), vm(2, half_terms, tall),
        vm(lines, half_terms, 2 * columns), vm(lines, half_terms, 2 * columns),
        vm(lines, half_terms, 2 * columns),
        vm(lines, BLOCK, 2 * columns), vm(lines, BLOCK, 2 * columns),
        vm(lines, 2 * BLOCK, columns), vm(lines, 2 * BLOCK, columns),
        vm(lines, BLOCK, columns), vm(lines, BLOCK, columns),
        vm(lines, 2 * BLOCK, columns), vm(lines + 1, 2 * BLOCK, columns),
        vm(lines, BLOCK, columns), vm(lines + 1, BLOCK, columns),
        vm(BLOCK, columns, dtype=f32), vm(2 * BLOCK, columns, dtype=f32), vm(LEN, 1, dtype=f32),
        vm(BLOCK, columns), vm(2 * BLOCK, columns),
        vm(3, BLOCK, columns), vm(2 * BLOCK, columns),
        vm(LEN, width, dtype=f32), vm(n, 1, columns, dtype=f32), vm(1, columns, dtype=f32),
        vm(n, 1, columns, dtype=f32), vm(1, columns, dtype=f32), vm(4, 1, columns, dtype=f32),
        pltpu.SemaphoreType.DMA, pltpu.SemaphoreType.DMA, pltpu.SemaphoreType.DMA((SEQ_DEV,)),
    ]
    scratch += pair(GATHER_GROUPS, lines) + pair(n) + pair(2) + pair(n)
    scratch += pair(3, lines) + pair(5, lines + 1) + pair(5) + pair(n) + pair(4)
    return pl.pallas_call(
        lambda *refs: whole_kernel(n, *refs),
        name="splade_step",
        out_shape=(
            jax.ShapeDtypeStruct((1, 128), f32),
            jax.ShapeDtypeStruct((tall, width), bf16),
            jax.ShapeDtypeStruct((terms, columns), f32),
            jax.ShapeDtypeStruct((1, columns), f32),
        ),
        in_specs=[ANY, VMEM, ANY, SMEM, SMEM, VMEM, VMEM],
        out_specs=(VMEM, ANY, VMEM, VMEM),
        scratch_shapes=scratch,
        compiler_params=pltpu.CompilerParams(
            collective_id=0, has_side_effects=True, vmem_limit_bytes=62 << 20
        ),
    )(piece, gain, tokens, lens, slots, triples, teacher)


def hand_kernel(cuts, *refs):
    count = len(cuts)
    ins, outs, held = refs[:count], refs[count : 2 * count], refs[2 * count : 3 * count]
    load_sem, store_sem = refs[3 * count :]
    loads, stores = [], []
    for src, dst, buffer, cut in zip(ins, outs, held, cuts):
        rows = src.shape[0] // cut
        for i in range(cut):
            spot, index = pl.ds(i * rows, rows), len(loads)
            loads.append(pltpu.make_async_copy(src.at[spot], buffer.at[spot], load_sem.at[index]))
            stores.append(pltpu.make_async_copy(buffer.at[spot], dst.at[spot], store_sem.at[index]))
    for load in loads:
        load.start()
    for load, store in zip(loads, stores):
        load.wait()
        store.start()
    for store in stores:
        store.wait()


def hand_out(*arrays):
    cuts = [max(1, x.size * x.dtype.itemsize >> 20) for x in arrays]
    return pl.pallas_call(
        lambda *refs: hand_kernel(cuts, *refs),
        name="hand_out",
        out_shape=tuple(jax.ShapeDtypeStruct(x.shape, x.dtype) for x in arrays),
        in_specs=[ANY] * len(arrays),
        out_specs=(ANY,) * len(arrays),
        scratch_shapes=[pltpu.VMEM(x.shape, x.dtype) for x in arrays]
        + [pltpu.SemaphoreType.DMA((sum(cuts),))] * 2,
        compiler_params=pltpu.CompilerParams(vmem_limit_bytes=62 << 20),
    )(*arrays)


def local(produced, lengths, active, window_blocks, triplets, teacher, norm_gain, head):
    shards = lax.axis_size("fsdp")
    columns = head.shape[1]
    piece = collect_rows(window_blocks, head)
    gain = norm_gain.reshape(columns // BLOCK, BLOCK)
    tokens = produced.reshape(SEQ_DEV * LEN, D)
    results = run_whole(
        piece, gain, tokens, lengths, active.transpose(1, 0, 2),
        triplets.transpose(2, 0, 1), teacher, shards,
    )
    loss_row, grad_tokens, head_grad, gain_grad = hand_out(*results)
    return (
        loss_row[0, :1],
        grad_tokens.reshape(1, SEQ_DEV, LEN, D),
        head_grad,
        gain_grad.reshape(columns),
    )


def solution(mesh):
    return jax.shard_map(
        local,
        mesh=mesh,
        in_specs=(
            P("section", "fsdp", None, None),
            P("section", "fsdp"),
            P("section", "fsdp", None),
            P(),
            P("section", None, None),
            P("section", None),
            P("fsdp"),
            P(None, "fsdp"),
        ),
        out_specs=(P("section"), P("section", "fsdp", None, None), P(None, "fsdp"), P("fsdp")),
        check_vma=False,
    )
```
